32 devices in a mesh: body: 16 (over z, y, x), brick: 2 (over core).
Axes of the slice: x: 2, y: 2, z: 4, core: 2. Of those that a mesh axis runs over, the one named last changes fastest.
Arguments:
- blob_force: float32 [3, 8, 98304], P(None, 'brick', 'body'), may hold values from -24 to 24
- blob_offset: float32 [3, 8, 98304], P(None, 'brick', 'body'), may hold values from -2.4 to 2.4
- patch_anchor: float32 [3, 8, 1024], P(None, 'brick', 'body'), may hold values from 2.4 to 5.6
- patch_count: int32 [1024, 8], P('body', 'brick'), may hold values from 1 to 96, 642 in all within a row
- block_owner: int32 [8, 1024, 1], P('brick', 'body'), may hold values from 0 to 31; in each aligned block of 64 rows (0 to 63, 64 to 127, ..., all dimensions but the last counted through in order) at most 4 rows name the same one
- block_tile: int32 [8, 1024], P('brick', 'body'), may hold values from 0 to 31
- body_mobility: float32 [6, 6, 1024], P(None, None, 'body'), may hold values from -0.015 to 0.015
Outputs:
- blob_velocity: float32 [3, 8, 98304], P(None, 'brick', 'body')
- grid_force: float32 [1024, 3, 512], P(('body', 'brick'))
The draws below stay inside these ranges and needn't reach their ends.
Inputs may be any that keep to these rules, and one draw needn't show every extreme that they name: `block_owner`: among the 64 patches of one patch index on one index of body (one aligned block of rows), at most 4 name the same owner, a bound that some block reaches. `patch_count`: the 8 counts of each body sum to 642.
All inputs are finite; a program needn't handle non-finite values. No bound on the sum of `patch_count` on one device may be relied on, other than what follows from the above.
Results may differ from the reference program's by a relative error of at most 0.0001.
Values sent between devices are 32-bit elements; how exact they have to be, the bound alone decides.
A program may use at most 64 MiB of HBM per device.

```python
import math
import jax
import jax.numpy as jnp
import numpy as np
from jax import lax

BLOBS = 642
PATCH = 8
PSLOT = 96
TILE_EDGE = 8
TILES_DEV = 32
BODY_GRP = 64
BODIES = 1024
CAP = 4
TILES = 1024
N_BODY = 16
DEVICES = 32


def touch_ends(result, key, least, high):
    longest = result.shape.index(max(result.shape))
    spots = []
    for shift in (0, 1):
        where = [jax.random.randint(jax.random.fold_in(key, axis), (), 0, length) for axis, length in enumerate(result.shape)]
        where[longest] = (where[longest] + shift) % result.shape[longest]
        spots.append(tuple(where))
    return result.at[spots[0]].set(least).at[spots[1]].set(high)


def steps_of(own_key, shape, cuts, least, largest):
    gain = 1.0
    for dim, parts in cuts:
        steps = jax.random.uniform(jax.random.fold_in(jax.random.fold_in(own_key, 6), dim), (parts,), jnp.float32, least / len(cuts), largest / len(cuts))
        gain = gain * jnp.repeat(jnp.exp(steps), shape[dim] // parts).reshape((-1,) + (1,) * (len(shape) - 1 - dim))
    return gain


def split_up(number_of, total, limit, slope):
    loads = [(1 << 20) // math.isqrt(standing ** slope) + 1 for standing in range(2, number_of + 1)]
    spare, counts = total - limit - (number_of - 1), [1] * (number_of - 1)
    while spare > 0:
        free = [i for i in range(number_of - 1) if counts[i] < limit]
        pool, left = sum([loads[i] for i in free]), spare
        for i in free:
            extra = min(limit - counts[i], max(1, left * loads[i] // pool), spare)
            counts[i] = counts[i] + extra
            spare = spare - extra
    return np.array([limit] + counts)


def uneven_parts(key, count, total, reach, skew):
    if count == 2:
        one = jax.random.randint(key, (), max(1, total - reach), min(reach, total - 1) + 1)
        return jnp.stack([one, total - one])
    tallies = jnp.asarray(split_up(count, total, reach, skew), jnp.int32)
    twos = (count - 1) // 2
    donor, receiver = tallies[1:1 + 2 * twos:2], tallies[2:2 + 2 * twos:2]
    slack = jnp.minimum(donor - 1, reach - receiver)
    moved = jax.random.randint(jax.random.fold_in(key, 1), (twos,), 0, 1 << 20) % (slack + 1)
    tallies = tallies.at[1:1 + 2 * twos:2].set(donor - moved).at[2:2 + 2 * twos:2].set(receiver + moved)
    return tallies[jax.random.permutation(jax.random.fold_in(key, 2), count)]


def assign_block(own_key, own, number, rows, amount, top, reach, slope):
    order = jax.random.permutation(own_key, amount)
    heavy_load, ordinary = load_shares(amount, rows * top, reach, slope, True), load_shares(amount, rows * top, reach, slope, False)
    places = jnp.arange(amount)

    def named(sizes, turn):
        used = int((sizes > 0).sum())
        fixed = max(1, used // 4)
        passed = fixed + (places - fixed + turn * (used - fixed)) % max(1, amount - fixed)
        return jnp.zeros((amount,), jnp.int32).at[order[jnp.where(places < fixed, places, passed)]].set(jnp.asarray(sizes, jnp.int32))

    sizes = jnp.where(number % 4 == 0, named(heavy_load, number // 4), named(ordinary, number - number // 4 - 1))
    mixed = jax.random.permutation(jax.random.fold_in(own, 3), amount)
    giver, sink = mixed[0:amount // 2 * 2:2], mixed[1:amount // 2 * 2:2]
    room = jnp.minimum(sizes[giver] - 1, reach - sizes[sink]) // 2
    room = jnp.where((giver == order[0]) | (sink == order[0]) | (sizes[sink] == 0), 0, jnp.maximum(room, 0))
    passed = jax.random.randint(jax.random.fold_in(own, 4), (amount // 2,), 0, 1 << 20) % (room + 1)
    sizes = sizes.at[giver].add(-passed).at[sink].add(passed)
    labels = jnp.searchsorted(jnp.cumsum(sizes), jnp.arange(rows * top), side="right").astype(jnp.int32)
    table = labels.reshape(top, rows).T
    table = table[jax.random.permutation(jax.random.fold_in(own, 1), rows)]
    turn = jax.random.randint(jax.random.fold_in(own, 2), (rows, 1), 0, top)
    return jnp.take_along_axis(table, (jnp.arange(top)[None, :] + turn) % top, axis=1)


def load_shares(amount, total, limit, lean, full):
    loads = [(1 << 20) // math.isqrt(standing ** lean) + 1 for standing in range(1, amount + 1)]
    largest = limit if full else min(limit, max(-(-total // amount), total * loads[0] // sum(loads)))
    least = 1 if total - largest >= amount - 1 else 0
    counts, spare = [largest] + [least] * (amount - 1), total - largest - least * (amount - 1)
    while spare > 0:
        candidates = [i for i in range(1, amount) if counts[i] < largest] or [i for i in range(1, amount) if counts[i] < limit]
        mass, budget = sum([loads[i] for i in candidates]), spare
        for i in candidates:
            more = min(limit - counts[i], max(1, budget * loads[i] // mass), spare)
            counts[i] = counts[i] + more
            spare = spare - more
    return np.array(counts)


def gaussian(own_key, dims, deviation, bound, shards=(), kind=jnp.bfloat16):
    values = deviation * jax.random.normal(own_key, dims, jnp.float32)
    if shards:
        values = values * steps_of(own_key, dims, shards, -0.22, 0.18)
    return jnp.clip(values, -bound, bound).astype(kind)


def setup_inputs(seed: int = 0) -> dict:
    streams_of = jax.random.split(jax.random.key(seed), 8)
    blob_force = gaussian(streams_of[0], (3, PATCH, BODIES * PSLOT), 4.0, 24.0, ((1, 2), (2, 16)), jnp.float32)
    blob_offset = jnp.clip(jax.random.uniform(streams_of[1], (3, PATCH, BODIES * PSLOT), jnp.float32, -2.4, 2.4) * steps_of(streams_of[1], (3, PATCH, BODIES * PSLOT), ((1, 2), (2, 16)), -0.4, 0.0), -2.4, 2.4)
    patch_anchor = jnp.clip(2.4 + 3.1999998 * jax.random.uniform(streams_of[2], (3, PATCH, BODIES), jnp.float32) ** steps_of(streams_of[2], (3, PATCH, BODIES), ((1, 2), (2, 16)), -0.2, 0.2), 2.4, 5.6)
    patch_count = jax.vmap(lambda own: uneven_parts(own, PATCH, BLOBS, PSLOT, 1))(jax.random.split(streams_of[3], BODIES)).reshape((BODIES, PATCH)).astype(jnp.int32)
    block_owner_keys = jax.random.split(jax.random.fold_in(streams_of[4], 1), PATCH * BODIES // BODY_GRP)
    block_owner_turns = jax.random.permutation(jax.random.fold_in(streams_of[4], 3), PATCH * BODIES // BODY_GRP)
    block_owner = jax.vmap(lambda own, number: assign_block(jax.random.fold_in(streams_of[4], 2), own, number, BODY_GRP, DEVICES, 1, CAP, 2))(block_owner_keys, block_owner_turns).reshape((PATCH, BODIES, 1))
    block_tile = touch_ends(jax.random.randint(streams_of[5], (PATCH, BODIES), 0, TILES_DEV), jax.random.fold_in(streams_of[5], 1), 0, TILES_DEV - 1).astype(jnp.int32)
    body_mobility = gaussian(streams_of[6], (6, 6, BODIES), 0.0025, 0.015, ((2, 16),), jnp.float32)
    return dict(blob_force=blob_force, blob_offset=blob_offset, patch_anchor=patch_anchor, patch_count=patch_count, block_owner=block_owner, block_tile=block_tile, body_mobility=body_mobility)


root_two_pi = math.sqrt(2.0 * math.pi)

def kernel_rows(coord, edge):
    centres = jnp.arange(edge, dtype=jnp.float32) + 0.5
    gap = coord[..., None] - centres
    return jnp.exp(-0.5 * gap * gap) / root_two_pi

def cross_rows(left, right):
    return jnp.stack([left[1] * right[2] - left[2] * right[1], left[2] * right[0] - left[0] * right[2], left[0] * right[1] - left[1] * right[0]])

def spread_blocks(forced, position, edge):
    wx = kernel_rows(position[0], edge)
    wy = kernel_rows(position[1], edge)
    wz = kernel_rows(position[2], edge)
    dense = wx[:, :, :, None, None] * wy[:, :, None, :, None]
    dense = dense * wz[:, :, None, None, :]
    count = forced.shape[1]
    dense = dense.reshape(count, forced.shape[2], edge ** 3)
    return jnp.einsum('cnp,npt->nct', forced, dense, precision=lax.Precision.HIGHEST)

def reference(blob_force, blob_offset, patch_anchor, patch_count, block_owner, block_tile, body_mobility):
    edge = TILE_EDGE
    cells = edge ** 3
    force = blob_force.reshape(3, PATCH, BODIES, PSLOT)
    offset = blob_offset.reshape(3, PATCH, BODIES, PSLOT)
    slot_ids = jnp.arange(PSLOT, dtype=jnp.int32)
    live = (slot_ids[None, None, :] < jnp.transpose(patch_count)[:, :, None]).astype(jnp.float32)
    loaded = force * live
    torque = cross_rows(offset, loaded)
    wrench = jnp.concatenate([lax.optimization_barrier(jnp.sum(loaded, axis=(1, 3))), lax.optimization_barrier(jnp.sum(torque, axis=(1, 3)))])
    velocity = lax.optimization_barrier(jnp.sum(body_mobility * wrench[None], axis=1))
    linear = velocity[0:3][:, None, :, None]
    angular = velocity[3:6][:, None, :, None]
    blob_velocity = (linear + cross_rows(angular, offset)) * live
    blob_velocity = blob_velocity.reshape(3, PATCH, BODIES * PSLOT)
    position = patch_anchor[:, :, :, None] + offset
    target = block_owner[:, :, 0] * TILES_DEV + block_tile
    pieces = PATCH * N_BODY
    force_pieces = loaded.reshape(3, pieces, BODY_GRP, PSLOT)
    place_pieces = position.reshape(3, pieces, BODY_GRP, PSLOT)
    target_pieces = target.reshape(pieces, BODY_GRP)

    def step(grid, index):
        share = spread_blocks(force_pieces[:, index], place_pieces[:, index], edge)
        share = share.reshape(BODY_GRP, 3 * cells)
        return (grid.at[target_pieces[index]].add(share), None)
    start = jnp.zeros((TILES, 3 * cells), jnp.float32)
    grid, _ = lax.scan(step, start, jnp.arange(pieces, dtype=jnp.int32))
    return (blob_velocity, grid.reshape(TILES, 3, cells))
```

```python
import functools
import math

import jax
import jax.numpy as jnp
import ml_dtypes
import numpy as np
from jax import lax
from jax.experimental import pallas as pl
from jax.experimental.pallas import tpu as pltpu
from jax.sharding import PartitionSpec as P

PSLOT = 96
TILE_EDGE = 8
TILES_DEV = 32
LOG_ROOT = 0.5 * math.log2(2.0 * math.pi)
HALF_LOG = 0.5 / math.log(2.0)
MESH = pl.DeviceIdType.MESH
NT = (((1,), (1,)), ((), ()))
F32 = jnp.float32
BF16 = jnp.bfloat16


def split3(x):
    hi = x.astype(BF16)
    rest = x - hi.astype(F32)
    mid = rest.astype(BF16)
    lo = (rest - mid.astype(F32)).astype(BF16)
    return hi, mid, lo


def stack3(x):
    hi = x.astype(BF16).astype(F32)
    rest = x - hi
    mid = rest.astype(BF16).astype(F32)
    lo = rest - mid
    return jnp.concatenate([hi, mid, lo], axis=0).astype(BF16)


def cross(left, right):
    return (
        left[1] * right[2] - left[2] * right[1],
        left[2] * right[0] - left[0] * right[2],
        left[0] * right[1] - left[1] * right[0],
    )


def segment_matrix(group, width, base):
    lane = lax.broadcasted_iota(jnp.int32, (group, width), 1) + base
    start = lax.broadcasted_iota(jnp.int32, (group, width), 0) * PSLOT
    gap = lane - start
    return jnp.where((gap >= 0) & (gap < PSLOT), 1.0, 0.0).astype(BF16)


def exponent_basis(edge):
    cells = edge * edge
    centre = np.arange(edge, dtype=np.float32) + 0.5 - edge / 2
    first = np.repeat(centre, edge)
    second = np.tile(centre, edge)
    basis = np.zeros((80, 8, cells), np.float32)
    for slot in range(8):
        for part in range(3):
            basis[8 * part + slot, slot] = 1.0
            basis[24 + 8 * part + slot, slot] = first
            basis[48 + 8 * part + slot, slot] = second
    rest = (-HALF_LOG * (first**2 + second**2)).astype(np.float32)
    for part in range(3):
        top = rest.astype(ml_dtypes.bfloat16).astype(np.float32)
        basis[72 + part, :] = top
        rest = rest - top
    return basis.reshape(80, 8 * cells).astype(ml_dtypes.bfloat16)


def step_kernel(
    dims,
    force_ref,
    offset_ref,
    anchor_ref,
    count_ref,
    owner_ref,
    tile_ref,
    mob_ref,
    basis_ref,
    vel_ref,
    grid_ref,
    rows_s,
    meta_s,
    live_s,
    flat_s,
    turn_s,
    data_s,
    split_s,
    send_s,
    ids_s,
    recv_s,
    ids_recv_s,
    comp_s,
    share_s,
    total_s,
    wr_s,
    wrecv_s,
    far_s,
    far_recv_s,
    send_sem,
    recv_sem,
    ids_send_sem,
    ids_recv_sem,
    wr_send_sem,
    wr_recv_sem,
    far_send_sem,
    far_recv_sem,
):
    bodies, bricks, lp, group, width, slots, tiles = dims
    n = bodies * bricks
    h = n // 2
    turn = h // 2 if h % 2 == 0 else 0
    length = group * PSLOT
    chunks = length // width
    per = width // PSLOT
    rpad = rows_s.shape[0]
    blocks = lp * group
    my_body = lax.axis_index("body")
    my_brick = lax.axis_index("brick")
    me = my_body * bricks + my_brick
    my_half = me // h
    mine = lax.rem(me, h)

    def device(half, place):
        d = half * h + place
        return (d // bricks, lax.rem(d, bricks))

    mirror = device(1 - my_half, lax.rem(mine + turn, h))

    barrier = pltpu.get_barrier_semaphore()

    def greet(k, carry):
        pl.semaphore_signal(
            barrier,
            inc=1,
            device_id=device(my_half, lax.rem(mine + k, h)),
            device_id_type=MESH,
        )
        return carry

    pl.semaphore_signal(barrier, inc=1, device_id=mirror, device_id_type=MESH)
    lax.fori_loop(1, h, greet, 0)

    rows_s[...] = jnp.zeros_like(rows_s)
    for c in range(3):
        rows_s[c * lp : (c + 1) * lp, :] = anchor_ref[c] - TILE_EDGE / 2
    starts = PSLOT * lax.broadcasted_iota(jnp.int32, (lp, group), 1)
    rows_s[3 * lp : 4 * lp, :] = (count_ref[...] + starts).astype(F32)
    for q in range(lp):
        meta_s[0:1, q * group : (q + 1) * group] = owner_ref[q]
        meta_s[1:2, q * group : (q + 1) * group] = tile_ref[q : q + 1, :]
    rows3 = stack3(rows_s[...])

    def chunk(j, carry):
        base = pl.multiple_of(j * width, 128)
        seg = segment_matrix(group, width, base)
        flat3 = jnp.dot(rows3, seg, preferred_element_type=F32)
        flat = flat3[0:rpad] + flat3[rpad : 2 * rpad] + flat3[2 * rpad : 3 * rpad]
        lane = (lax.broadcasted_iota(jnp.int32, (lp, width), 1) + base).astype(F32)
        live = jnp.where(lane < flat[3 * lp : 4 * lp], 1.0, 0.0)
        live_s[:, pl.ds(base, width)] = live
        loaded = [force_ref[c, :, pl.ds(base, width)] * live for c in range(3)]
        offset = [offset_ref[c, :, pl.ds(base, width)] for c in range(3)]
        for c in range(3):
            flat_s[c] = loaded[c]
            flat_s[3 + c] = offset[c] + flat[c * lp : (c + 1) * lp]
        for m in range(per):
            for c in range(6):
                piece = flat_s[c, :, m * PSLOT : (m + 1) * PSLOT]
                for q in range(lp):
                    turn_s[q, m : m + 1, c * PSLOT : (c + 1) * PSLOT] = piece[q : q + 1]
        data_s[:, pl.ds(pl.multiple_of(j * per, per), per), :] = turn_s[...]
        return carry

    lax.fori_loop(0, chunks, chunk, 0, unroll=8)

    data = data_s[...].reshape(blocks, 640)
    tail = data[:, 512:576]
    hi, mid, lo = split3(jnp.concatenate([data[:, 0:512], tail, tail], axis=1))
    split_s[0] = hi
    split_s[1] = mid
    split_s[2] = lo

    owner = meta_s[0:1, :]
    tile = meta_s[1:2, :]
    place = lax.rem(owner, h)
    proxy = place + turn
    proxy = jnp.where(proxy >= h, proxy - h, proxy)
    owner = jnp.where(owner // h == my_half, place + h, proxy)
    is_owner = lax.broadcasted_iota(jnp.int32, (n, blocks), 0) == owner
    hot = jnp.where(is_owner, 1.0, 0.0)
    before = jnp.where(
        lax.broadcasted_iota(jnp.int32, (blocks, blocks), 0)
        < lax.broadcasted_iota(jnp.int32, (blocks, blocks), 1),
        1.0,
        0.0,
    ).astype(BF16)
    seen = jnp.dot(hot.astype(BF16), before, preferred_element_type=F32)
    rank = jnp.sum(hot * seen, axis=0, keepdims=True)
    rank = (rank + 0.5).astype(jnp.int32)
    lane_of = rank // 2 + 64 * lax.rem(rank, 2)
    rank_hot = jnp.where(
        lax.broadcasted_iota(jnp.int32, (128, blocks), 0) == lane_of, 1.0, 0.0
    ).astype(BF16)
    weighted = (hot * tile.astype(F32)).astype(BF16)
    ids = lax.dot_general(weighted, rank_hot, NT, preferred_element_type=F32)
    ids_s[:, 0, :] = (ids + 0.5).astype(jnp.int32)
    slot_of = owner * slots + rank

    dest_blk = max(1, 128 // slots)
    while h % dest_blk:
        dest_blk //= 2
    rows = dest_blk * slots
    planes = h // dest_blk
    my_plane = mine // dest_blk
    my_place = lax.rem(mine, dest_blk)

    def plane_of(g):
        if planes & (planes - 1):
            return lax.rem(my_plane + g, planes)
        total = jnp.int32(0)
        bit = 1
        while bit < planes:
            total = total + lax.rem(my_plane // bit + g // bit, 2) * bit
            bit *= 2
        return total

    def dest_of(g, j):
        return plane_of(g) * dest_blk + lax.rem(my_place + j, dest_blk)


    pl.semaphore_wait(barrier, h)

    def wr_copy(k):
        other = lax.rem(my_brick + k, bricks)
        return pltpu.make_async_remote_copy(
            src_ref=wr_s,
            dst_ref=wrecv_s.at[my_brick],
            send_sem=wr_send_sem.at[k],
            recv_sem=wr_recv_sem.at[k],
            device_id=(my_body, other),
            device_id_type=MESH,
        )

    def start(phase, k, carry):
        d = dest_of(k // dest_blk, lax.rem(k, dest_blk))
        where = device(my_half, d)
        slot = phase * h + k
        pltpu.make_async_remote_copy(
            src_ref=send_s.at[slot],
            dst_ref=recv_s.at[slot],
            send_sem=send_sem.at[phase],
            recv_sem=recv_sem.at[slot],
            device_id=where,
            device_id_type=MESH,
        ).start()
        pltpu.make_async_remote_copy(
            src_ref=ids_s.at[phase * h + d],
            dst_ref=ids_recv_s.at[slot],
            send_sem=ids_send_sem.at[phase],
            recv_sem=ids_recv_sem.at[slot],
            device_id=where,
            device_id_type=MESH,
        ).start()
        return carry

    def pack(i, carry):
        phase = i // planes
        g = lax.rem(i + 1, planes)
        place = lax.broadcasted_iota(jnp.int32, (rows, blocks), 0) + my_place * slots
        place = jnp.where(place >= rows, place - rows, place)
        target = phase * (h * slots) + plane_of(g) * rows + place
        pick = jnp.where(target == slot_of, 1.0, 0.0).astype(BF16)
        out = jnp.dot(pick, split_s[0], preferred_element_type=F32)
        out = out + jnp.dot(pick, split_s[1], preferred_element_type=F32)
        out = out + jnp.dot(pick, split_s[2], preferred_element_type=F32)
        low = lax.broadcasted_iota(jnp.int32, (8, 128), 1) < 64
        nch = slots // 8
        for d in range(dest_blk):
            k = phase * h + g * dest_blk + d
            for m in range(nch):
                r = d * slots + m * 8
                for t in range(4):
                    send_s[k, m * 4 + t] = out[r : r + 8, t * 128 : (t + 1) * 128]
            if nch % 2 == 0:
                for m in range(0, nch, 2):
                    r = d * slots + m * 8
                    send_s[k, 4 * nch + m // 2] = jnp.where(
                        low, out[r : r + 8, 512:640], out[r + 8 : r + 16, 512:640]
                    )
            else:
                for m in range(nch):
                    r = d * slots + m * 8
                    send_s[k, 4 * nch + m] = out[r : r + 8, 512:640]

        least = jnp.where(g == 0, 1, 0)
        lax.fori_loop(
            g * dest_blk + least, (g + 1) * dest_blk, functools.partial(start, phase), 0
        )
        return carry

    def own_copies(phase):
        k = phase * h
        return (
            pltpu.make_async_copy(send_s.at[k], recv_s.at[k], recv_sem.at[k]),
            pltpu.make_async_copy(ids_s.at[k + mine], ids_recv_s.at[k], ids_recv_sem.at[k]),
        )

    lax.fori_loop(0, 2 * planes, pack, 0)
    for phase in range(2):
        for copy in own_copies(phase):
            copy.start()

    def wrench_part(j, wrench):
        base = pl.multiple_of(j * width, 128)
        seg = segment_matrix(group, width, base)
        live = live_s[:, pl.ds(base, width)]
        loaded = [force_ref[c, :, pl.ds(base, width)] * live for c in range(3)]
        offset = [offset_ref[c, :, pl.ds(base, width)] for c in range(3)]
        torque = cross(offset, loaded)
        sums = [jnp.sum(v, axis=0, keepdims=True) for v in loaded + list(torque)]
        sums = jnp.concatenate(sums + [jnp.zeros((2, width), F32)], axis=0)
        return wrench + lax.dot_general(stack3(sums), seg, NT, preferred_element_type=F32)

    wrench3 = lax.fori_loop(0, chunks, wrench_part, jnp.zeros((24, group), F32), unroll=8)
    wr_s[...] = wrench3[0:8] + wrench3[8:16] + wrench3[16:24]
    wrecv_s[my_brick] = wr_s[...]
    for k in range(1, bricks):
        wr_copy(k).start()

    def velocities():
        for k in range(1, bricks):
            wr_copy(k).wait()
        wrench = wrecv_s[0]
        for k in range(1, bricks):
            wrench = wrench + wrecv_s[k]
        velocity = [jnp.sum(mob_ref[i] * wrench[0:6], axis=0, keepdims=True) for i in range(6)]
        velocity = jnp.concatenate(velocity + [jnp.zeros((2, group), F32)], axis=0)
        vel3 = stack3(velocity)

        def spread_velocity(j, carry):
            base = pl.multiple_of(j * width, 128)
            seg = segment_matrix(group, width, base)
            v3 = jnp.dot(vel3, seg, preferred_element_type=F32)
            v = v3[0:8] + v3[8:16] + v3[16:24]
            live = live_s[:, pl.ds(base, width)]
            offset = [offset_ref[c, :, pl.ds(base, width)] for c in range(3)]
            spin = cross([v[3:4], v[4:5], v[5:6]], offset)
            for c in range(3):
                vel_ref[c, :, pl.ds(base, width)] = (v[c : c + 1] + spin[c]) * live
            return carry

        lax.fori_loop(0, chunks, spread_velocity, 0, unroll=8)

    nch = slots // 8
    edge = TILE_EDGE
    rows_ci = 3 * edge
    batch = dest_blk
    lanes8 = lax.broadcasted_iota(jnp.int32, (8, 128), 1)
    centre = lax.broadcasted_iota(jnp.int32, (edge, 128), 0).astype(F32) + (0.5 - edge / 2)
    pairs = slots // 2
    low_share = lax.broadcasted_iota(jnp.int32, (rows_ci, 128), 1) < edge * edge
    low = lax.broadcasted_iota(jnp.int32, (TILES_DEV, 128), 1) < edge * edge

    blank = jnp.zeros((128 - PSLOT, 4 * edge * edge), BF16)

    def unpacked(k, m):
        parts = [recv_s[k, 4 * m + t] for t in range(4)]
        if nch % 2 == 0:
            tail = recv_s[k, 4 * nch + m // 2]
            if m % 2:
                tail = pltpu.roll(tail, 64, 1)
        else:
            tail = recv_s[k, 4 * nch + m]
        parts.append(tail)
        values = []
        for c in range(6):
            first, off = divmod(c * PSLOT, 128)
            value = parts[first]
            if off:
                value = pltpu.roll(value, 128 - off, 1)
                if off + PSLOT > 128:
                    other = pltpu.roll(parts[first + 1], 128 - off, 1)
                    value = jnp.where(lanes8 < 128 - off, value, other)
            values.append(value)
        return values

    def features_of(y, z):
        level = -2.0 * LOG_ROOT - HALF_LOG * (y * y + z * z)
        features = []
        for value in (level, (2.0 * HALF_LOG) * y, (2.0 * HALF_LOG) * z):
            top = value.astype(BF16).astype(F32)
            rest = value - top
            middle = rest.astype(BF16).astype(F32)
            features += [top, middle, rest - middle]
        features.append(jnp.ones((8, 128), F32))
        features = jnp.concatenate(features, axis=0).astype(BF16)
        return jnp.swapaxes(features, 0, 1)[0:PSLOT]

    def left_of(m, r):
        row = [comp_s[m, c, r : r + 1, :] for c in range(4)]
        gap = row[3] - centre
        wx = jnp.exp2(-LOG_ROOT - HALF_LOG * (gap * gap))
        return [row[c] * wx for c in range(3)]

    def shares(k):
        values = [unpacked(k, m) for m in range(nch)]
        for m in range(nch):
            for c in range(4):
                comp_s[m, c] = values[m][c]
        features = jnp.concatenate([features_of(v[4], v[5]) for v in values], axis=0)
        exponent = jnp.dot(features, basis_ref[...], preferred_element_type=F32)
        for m in range(nch):
            for half in range(2):
                lanes = slice(half * 256, (half + 1) * 256)
                right = jnp.exp2(exponent[m * PSLOT : (m + 1) * PSLOT, lanes])
                right_hi = right.astype(BF16)
                right_lo = (right - right_hi.astype(F32)).astype(BF16)
                right = jnp.concatenate([right_hi, blank, right_lo, blank], axis=0)
                left = []
                for r in range(4 * half, 4 * half + 4):
                    left += left_of(m, r)
                left = jnp.concatenate(left, axis=0)
                left_hi = left.astype(BF16)
                left_lo = (left - left_hi.astype(F32)).astype(BF16)
                left = jnp.concatenate(
                    [
                        jnp.concatenate([left_hi, left_hi], axis=1),
                        jnp.concatenate([left_lo, jnp.zeros_like(left_lo)], axis=1),
                    ],
                    axis=0,
                )
                both = jnp.dot(left, right, preferred_element_type=F32)
                for t in range(2):
                    lanes = slice(t * 128, (t + 1) * 128)
                    at = 2 * t * rows_ci
                    even = both[at : at + rows_ci, lanes]
                    even = even + both[at + 4 * rows_ci : at + 5 * rows_ci, lanes]
                    odd = both[at + rows_ci : at + 2 * rows_ci, lanes]
                    odd = odd + both[at + 5 * rows_ci : at + 6 * rows_ci, lanes]
                    yield jnp.where(low_share, even, odd)

    def arrivals(g, carry):
        def sender(b, names):
            k = g * batch + b
            pltpu.make_async_copy(recv_s.at[k], recv_s.at[k], recv_sem.at[k]).wait()
            pltpu.make_async_copy(ids_recv_s.at[k], ids_recv_s.at[k], ids_recv_sem.at[k]).wait()
            for t, share in enumerate(shares(k)):
                at = pl.multiple_of((b * pairs + t) * rows_ci, 8)
                share_s[pl.ds(at, rows_ci), :] = share
            return names

        lax.fori_loop(0, batch, sender, 0, unroll=8)
        count = batch * pairs
        names = jnp.zeros((1, 128), jnp.int32)
        for b in range(batch):
            row = ids_recv_s[g * batch + b]
            names = names + (pltpu.roll(row, b * pairs, 1) if b else row)
        tile_of = lax.broadcasted_iota(jnp.int32, (TILES_DEV, 128), 0)
        hot_tile = jnp.concatenate(
            [
                jnp.where(tile_of == names, 1.0, 0.0)[:, 0:count],
                jnp.where(tile_of == pltpu.roll(names, 64, 1), 1.0, 0.0)[:, 0:count],
            ],
            axis=0,
        ).astype(BF16)
        for r in range(rows_ci):
            share = share_s[pl.ds(r, count, stride=rows_ci), :]
            share_hi = share.astype(BF16)
            share_lo = (share - share_hi.astype(F32)).astype(BF16)
            gained = jnp.dot(hot_tile, share_hi, preferred_element_type=F32)
            gained = gained + jnp.dot(hot_tile, share_lo, preferred_element_type=F32)
            total_s[r] = total_s[r] + jnp.where(low, gained[0:TILES_DEV], gained[TILES_DEV:])
        return carry

    def folded(c, i):
        even = total_s[c * edge + i]
        odd = total_s[c * edge + i + 1]
        even = even + pltpu.roll(even, 64, 1)
        odd = odd + pltpu.roll(odd, 64, 1)
        return jnp.where(low, even, odd)

    far = pltpu.make_async_remote_copy(
        src_ref=far_s,
        dst_ref=far_recv_s,
        send_sem=far_send_sem,
        recv_sem=far_recv_sem,
        device_id=mirror,
        device_id_type=MESH,
    )
    total_s[...] = jnp.zeros_like(total_s)
    lax.fori_loop(0, planes, arrivals, 0)
    for c in range(3):
        for i in range(0, edge, 2):
            far_s[c, :, i * 64 : i * 64 + 128] = folded(c, i)
    far.start()
    velocities()
    total_s[...] = jnp.zeros_like(total_s)
    lax.fori_loop(planes, 2 * planes, arrivals, 0)
    far.wait()
    for c in range(3):
        for i in range(0, edge, 2):
            cells = slice(i * 64, i * 64 + 128)
            grid_ref[c, :, cells] = folded(c, i) + far_recv_s[c, :, cells]

    for phase in range(2):
        rest = send_s.at[pl.ds(phase * h + 1, h - 1)]
        pltpu.make_async_copy(rest, rest, send_sem.at[phase]).wait()
        rest_ids = ids_s.at[pl.ds(phase * h + 1, h - 1)]
        pltpu.make_async_copy(rest_ids, rest_ids, ids_send_sem.at[phase]).wait()


def body(
    blob_force, blob_offset, patch_anchor, patch_count, block_owner, block_tile, body_mobility
):
    edge = TILE_EDGE
    lp = blob_force.shape[1]
    group = body_mobility.shape[2]
    length = group * PSLOT
    bodies = lax.axis_size("body")
    bricks = lax.axis_size("brick")
    n = bodies * bricks
    capacity = max(2, 2 * group // n)
    slots = -(-lp * capacity // 8) * 8
    nch = slots // 8
    tiles = 4 * nch + (nch // 2 if nch % 2 == 0 else nch)
    blocks = lp * group
    width = 768
    rpad = -(-4 * lp // 8) * 8
    batch = max(1, 128 // slots)
    while (n // 2) % batch:
        batch //= 2
    dims = (bodies, bricks, lp, group, width, slots, tiles)
    vmem = pl.BlockSpec(memory_space=pltpu.VMEM)
    velocity, grid = pl.pallas_call(
        functools.partial(step_kernel, dims),
        name="step",
        out_shape=(
            jax.ShapeDtypeStruct((3, lp, length), F32),
            jax.ShapeDtypeStruct((3, TILES_DEV, edge**3), F32),
        ),
        in_specs=[vmem] * 8,
        out_specs=(vmem, vmem),
        scratch_shapes=[
            pltpu.VMEM((rpad, group), F32),
            pltpu.VMEM((2, blocks), jnp.int32),
            pltpu.VMEM((lp, length), F32),
            pltpu.VMEM((6, lp, width), F32),
            pltpu.VMEM((lp, 8, 640), F32),
            pltpu.VMEM((lp, group, 640), F32),
            pltpu.VMEM((3, blocks, 640), BF16),
            pltpu.VMEM((n, tiles, 8, 128), F32),
            pltpu.VMEM((n, 1, 128), jnp.int32),
            pltpu.VMEM((n, tiles, 8, 128), F32),
            pltpu.VMEM((n, 1, 128), jnp.int32),
            pltpu.VMEM((nch, 4, 8, 128), F32),
            pltpu.VMEM((batch * slots // 2 * 3 * edge, 128), F32),
            pltpu.VMEM((3 * edge, TILES_DEV, 128), F32),
            pltpu.VMEM((8, group), F32),
            pltpu.VMEM((bricks, 8, group), F32),
            pltpu.VMEM((3, TILES_DEV, edge**3), F32),
            pltpu.VMEM((3, TILES_DEV, edge**3), F32),
            pltpu.SemaphoreType.DMA((2,)),
            pltpu.SemaphoreType.DMA((n,)),
            pltpu.SemaphoreType.DMA((2,)),
            pltpu.SemaphoreType.DMA((n,)),
            pltpu.SemaphoreType.DMA((bricks,)),
            pltpu.SemaphoreType.DMA((bricks,)),
            pltpu.SemaphoreType.DMA,
            pltpu.SemaphoreType.DMA,
        ],
        compiler_params=pltpu.CompilerParams(
            collective_id=0, has_side_effects=True, vmem_limit_bytes=60 << 20
        ),
    )(
        blob_force,
        blob_offset,
        patch_anchor,
        jnp.transpose(patch_count),
        jnp.transpose(block_owner, (0, 2, 1)),
        block_tile,
        body_mobility,
        jnp.asarray(exponent_basis(edge)),
    )
    return velocity, jnp.transpose(grid, (1, 0, 2))


def solution(mesh):
    in_specs = (
        P(None, "brick", "body"),
        P(None, "brick", "body"),
        P(None, "brick", "body"),
        P("body", "brick"),
        P("brick", "body", None),
        P("brick", "body"),
        P(None, None, "body"),
    )
    out_specs = (P(None, "brick", "body"), P(("body", "brick"), None, None))
    return jax.shard_map(body, mesh=mesh, in_specs=in_specs, out_specs=out_specs, check_vma=False)
```

```python
import functools
import math

import jax
import jax.numpy as jnp
import ml_dtypes
import numpy as np
from jax import lax
from jax.experimental import pallas as pl
from jax.experimental.pallas import tpu as pltpu
from jax.sharding import PartitionSpec as P

PSLOT = 96
TILE_EDGE = 8
TILES_DEV = 32
LOG_ROOT = 0.5 * math.log2(2.0 * math.pi)
HALF_LOG = 0.5 / math.log(2.0)
MESH = pl.DeviceIdType.MESH
NT = (((1,), (1,)), ((), ()))
F32 = jnp.float32
BF16 = jnp.bfloat16


def split3(x):
    hi = x.astype(BF16)
    rest = x - hi.astype(F32)
    mid = rest.astype(BF16)
    lo = (rest - mid.astype(F32)).astype(BF16)
    return hi, mid, lo


def stack3(x):
    hi = x.astype(BF16).astype(F32)
    rest = x - hi
    mid = rest.astype(BF16).astype(F32)
    lo = rest - mid
    return jnp.concatenate([hi, mid, lo], axis=0).astype(BF16)


def cross(left, right):
    return (
        left[1] * right[2] - left[2] * right[1],
        left[2] * right[0] - left[0] * right[2],
        left[0] * right[1] - left[1] * right[0],
    )


def segment_matrix(group, width, base):
    lane = lax.broadcasted_iota(jnp.int32, (group, width), 1) + base
    start = lax.broadcasted_iota(jnp.int32, (group, width), 0) * PSLOT
    gap = lane - start
    return jnp.where((gap >= 0) & (gap < PSLOT), 1.0, 0.0).astype(BF16)


def exponent_basis(edge):
    cells = edge * edge
    centre = np.arange(edge, dtype=np.float32) + 0.5 - edge / 2
    first = np.repeat(centre, edge)
    second = np.tile(centre, edge)
    basis = np.zeros((80, 8, cells), np.float32)
    for slot in range(8):
        for part in range(3):
            basis[8 * part + slot, slot] = 1.0
            basis[24 + 8 * part + slot, slot] = first
            basis[48 + 8 * part + slot, slot] = second
    rest = (-HALF_LOG * (first**2 + second**2)).astype(np.float32)
    for part in range(3):
        top = rest.astype(ml_dtypes.bfloat16).astype(np.float32)
        basis[72 + part, :] = top
        rest = rest - top
    return basis.reshape(80, 8 * cells).astype(ml_dtypes.bfloat16)


def step_kernel(
    dims,
    force_ref,
    offset_ref,
    anchor_ref,
    count_ref,
    owner_ref,
    tile_ref,
    mob_ref,
    basis_ref,
    vel_ref,
    grid_ref,
    rows_s,
    meta_s,
    live_s,
    flat_s,
    turn_s,
    data_s,
    split_s,
    send_s,
    ids_s,
    recv_s,
    ids_recv_s,
    comp_s,
    feature_s,
    right_s,
    left_s,
    share_s,
    total_s,
    wr_s,
    wrecv_s,
    far_s,
    far_recv_s,
    send_sem,
    recv_sem,
    ids_send_sem,
    ids_recv_sem,
    wr_send_sem,
    wr_recv_sem,
    far_send_sem,
    far_recv_sem,
):
    bodies, bricks, lp, group, width, slots, tiles = dims
    n = bodies * bricks
    h = n // 2
    turn = h // 2 if h % 2 == 0 else 0
    length = group * PSLOT
    chunks = length // width
    per = width // PSLOT
    rpad = rows_s.shape[0]
    blocks = lp * group
    my_body = lax.axis_index("body")
    my_brick = lax.axis_index("brick")
    me = my_body * bricks + my_brick
    my_half = me // h
    mine = lax.rem(me, h)

    def device(half, place):
        d = half * h + place
        return (d // bricks, lax.rem(d, bricks))

    mirror = device(1 - my_half, lax.rem(mine + turn, h))

    barrier = pltpu.get_barrier_semaphore()

    def greet(k, carry):
        pl.semaphore_signal(
            barrier,
            inc=1,
            device_id=device(my_half, lax.rem(mine + k, h)),
            device_id_type=MESH,
        )
        return carry

    pl.semaphore_signal(barrier, inc=1, device_id=mirror, device_id_type=MESH)
    lax.fori_loop(1, h, greet, 0)

    rows_s[...] = jnp.zeros_like(rows_s)
    for c in range(3):
        rows_s[c * lp : (c + 1) * lp, :] = anchor_ref[c] - TILE_EDGE / 2
    starts = PSLOT * lax.broadcasted_iota(jnp.int32, (lp, group), 1)
    rows_s[3 * lp : 4 * lp, :] = (count_ref[...] + starts).astype(F32)
    for q in range(lp):
        meta_s[0:1, q * group : (q + 1) * group] = owner_ref[q]
        meta_s[1:2, q * group : (q + 1) * group] = tile_ref[q : q + 1, :]
    rows3 = stack3(rows_s[...])

    def chunk(j, carry):
        base = pl.multiple_of(j * width, 128)
        seg = segment_matrix(group, width, base)
        flat3 = jnp.dot(rows3, seg, preferred_element_type=F32)
        flat = flat3[0:rpad] + flat3[rpad : 2 * rpad] + flat3[2 * rpad : 3 * rpad]
        lane = (lax.broadcasted_iota(jnp.int32, (lp, width), 1) + base).astype(F32)
        live = jnp.where(lane < flat[3 * lp : 4 * lp], 1.0, 0.0)
        live_s[:, pl.ds(base, width)] = live
        loaded = [force_ref[c, :, pl.ds(base, width)] * live for c in range(3)]
        offset = [offset_ref[c, :, pl.ds(base, width)] for c in range(3)]
        for c in range(3):
            flat_s[c] = loaded[c]
            flat_s[3 + c] = offset[c] + flat[c * lp : (c + 1) * lp]
        for m in range(per):
            for c in range(6):
                piece = flat_s[c, :, m * PSLOT : (m + 1) * PSLOT]
                for q in range(lp):
                    turn_s[q, m : m + 1, c * PSLOT : (c + 1) * PSLOT] = piece[q : q + 1]
        data_s[:, pl.ds(pl.multiple_of(j * per, per), per), :] = turn_s[...]
        return carry

    lax.fori_loop(0, chunks, chunk, 0, unroll=8)

    data = data_s[...].reshape(blocks, 640)
    tail = data[:, 512:576]
    hi, mid, lo = split3(jnp.concatenate([data[:, 0:512], tail, tail], axis=1))
    split_s[0] = hi
    split_s[1] = mid
    split_s[2] = lo

    owner = meta_s[0:1, :]
    tile = meta_s[1:2, :]
    place = lax.rem(owner, h)
    proxy = place + turn
    proxy = jnp.where(proxy >= h, proxy - h, proxy)
    owner = jnp.where(owner // h == my_half, place + h, proxy)
    is_owner = lax.broadcasted_iota(jnp.int32, (n, blocks), 0) == owner
    hot = jnp.where(is_owner, 1.0, 0.0)
    before = jnp.where(
        lax.broadcasted_iota(jnp.int32, (blocks, blocks), 0)
        < lax.broadcasted_iota(jnp.int32, (blocks, blocks), 1),
        1.0,
        0.0,
    ).astype(BF16)
    seen = jnp.dot(hot.astype(BF16), before, preferred_element_type=F32)
    rank = jnp.sum(hot * seen, axis=0, keepdims=True)
    rank = (rank + 0.5).astype(jnp.int32)
    lane_of = rank // 2 + 64 * lax.rem(rank, 2)
    rank_hot = jnp.where(
        lax.broadcasted_iota(jnp.int32, (128, blocks), 0) == lane_of, 1.0, 0.0
    ).astype(BF16)
    weighted = (hot * tile.astype(F32)).astype(BF16)
    ids = lax.dot_general(weighted, rank_hot, NT, preferred_element_type=F32)
    ids_s[:, 0, :] = (ids + 0.5).astype(jnp.int32)
    slot_of = owner * slots + rank

    dest_blk = max(1, 128 // slots)
    while h % dest_blk:
        dest_blk //= 2
    rows = dest_blk * slots
    planes = h // dest_blk
    my_plane = mine // dest_blk
    my_place = lax.rem(mine, dest_blk)

    def plane_of(g):
        if planes & (planes - 1):
            return lax.rem(my_plane + g, planes)
        total = jnp.int32(0)
        bit = 1
        while bit < planes:
            total = total + lax.rem(my_plane // bit + g // bit, 2) * bit
            bit *= 2
        return total

    def dest_of(g, j):
        return plane_of(g) * dest_blk + lax.rem(my_place + j, dest_blk)


    pl.semaphore_wait(barrier, h)

    def wr_copy(k):
        other = lax.rem(my_brick + k, bricks)
        return pltpu.make_async_remote_copy(
            src_ref=wr_s,
            dst_ref=wrecv_s.at[my_brick],
            send_sem=wr_send_sem.at[k],
            recv_sem=wr_recv_sem.at[k],
            device_id=(my_body, other),
            device_id_type=MESH,
        )

    def start(phase, k, carry):
        d = dest_of(k // dest_blk, lax.rem(k, dest_blk))
        where = device(my_half, d)
        slot = phase * h + k
        pltpu.make_async_remote_copy(
            src_ref=send_s.at[slot],
            dst_ref=recv_s.at[slot],
            send_sem=send_sem.at[phase],
            recv_sem=recv_sem.at[slot],
            device_id=where,
            device_id_type=MESH,
        ).start()
        pltpu.make_async_remote_copy(
            src_ref=ids_s.at[phase * h + d],
            dst_ref=ids_recv_s.at[slot],
            send_sem=ids_send_sem.at[phase],
            recv_sem=ids_recv_sem.at[slot],
            device_id=where,
            device_id_type=MESH,
        ).start()
        return carry

    def pack(i, carry):
        phase = i // planes
        g = lax.rem(i + 1, planes)
        place = lax.broadcasted_iota(jnp.int32, (rows, blocks), 0) + my_place * slots
        place = jnp.where(place >= rows, place - rows, place)
        target = phase * (h * slots) + plane_of(g) * rows + place
        pick = jnp.where(target == slot_of, 1.0, 0.0).astype(BF16)
        out = jnp.dot(pick, split_s[0], preferred_element_type=F32)
        out = out + jnp.dot(pick, split_s[1], preferred_element_type=F32)
        out = out + jnp.dot(pick, split_s[2], preferred_element_type=F32)
        low = lax.broadcasted_iota(jnp.int32, (8, 128), 1) < 64
        nch = slots // 8
        for d in range(dest_blk):
            k = phase * h + g * dest_blk + d
            for m in range(nch):
                r = d * slots + m * 8
                for t in range(4):
                    send_s[k, m * 4 + t] = out[r : r + 8, t * 128 : (t + 1) * 128]
            if nch % 2 == 0:
                for m in range(0, nch, 2):
                    r = d * slots + m * 8
                    send_s[k, 4 * nch + m // 2] = jnp.where(
                        low, out[r : r + 8, 512:640], out[r + 8 : r + 16, 512:640]
                    )
            else:
                for m in range(nch):
                    r = d * slots + m * 8
                    send_s[k, 4 * nch + m] = out[r : r + 8, 512:640]

        least = jnp.where(g == 0, 1, 0)
        lax.fori_loop(
            g * dest_blk + least, (g + 1) * dest_blk, functools.partial(start, phase), 0
        )
        return carry

    def own_copies(phase):
        k = phase * h
        return (
            pltpu.make_async_copy(send_s.at[k], recv_s.at[k], recv_sem.at[k]),
            pltpu.make_async_copy(ids_s.at[k + mine], ids_recv_s.at[k], ids_recv_sem.at[k]),
        )

    lax.fori_loop(0, 2 * planes, pack, 0)
    for phase in range(2):
        for copy in own_copies(phase):
            copy.start()

    def wrench_part(j, wrench):
        base = pl.multiple_of(j * width, 128)
        seg = segment_matrix(group, width, base)
        live = live_s[:, pl.ds(base, width)]
        loaded = [force_ref[c, :, pl.ds(base, width)] * live for c in range(3)]
        offset = [offset_ref[c, :, pl.ds(base, width)] for c in range(3)]
        torque = cross(offset, loaded)
        sums = [jnp.sum(v, axis=0, keepdims=True) for v in loaded + list(torque)]
        sums = jnp.concatenate(sums + [jnp.zeros((2, width), F32)], axis=0)
        return wrench + lax.dot_general(stack3(sums), seg, NT, preferred_element_type=F32)

    wrench3 = lax.fori_loop(0, chunks, wrench_part, jnp.zeros((24, group), F32), unroll=8)
    wr_s[...] = wrench3[0:8] + wrench3[8:16] + wrench3[16:24]
    wrecv_s[my_brick] = wr_s[...]
    for k in range(1, bricks):
        wr_copy(k).start()

    def velocities():
        for k in range(1, bricks):
            wr_copy(k).wait()
        wrench = wrecv_s[0]
        for k in range(1, bricks):
            wrench = wrench + wrecv_s[k]
        velocity = [jnp.sum(mob_ref[i] * wrench[0:6], axis=0, keepdims=True) for i in range(6)]
        velocity = jnp.concatenate(velocity + [jnp.zeros((2, group), F32)], axis=0)
        vel3 = stack3(velocity)

        def spread_velocity(j, carry):
            base = pl.multiple_of(j * width, 128)
            seg = segment_matrix(group, width, base)
            v3 = jnp.dot(vel3, seg, preferred_element_type=F32)
            v = v3[0:8] + v3[8:16] + v3[16:24]
            live = live_s[:, pl.ds(base, width)]
            offset = [offset_ref[c, :, pl.ds(base, width)] for c in range(3)]
            spin = cross([v[3:4], v[4:5], v[5:6]], offset)
            for c in range(3):
                vel_ref[c, :, pl.ds(base, width)] = (v[c : c + 1] + spin[c]) * live
            return carry

        lax.fori_loop(0, chunks, spread_velocity, 0, unroll=8)

    nch = slots // 8
    edge = TILE_EDGE
    rows_ci = 3 * edge
    batch = dest_blk
    lanes8 = lax.broadcasted_iota(jnp.int32, (8, 128), 1)
    centre = lax.broadcasted_iota(jnp.int32, (edge, 128), 0).astype(F32) + (0.5 - edge / 2)
    pairs = slots // 2
    low_share = lax.broadcasted_iota(jnp.int32, (rows_ci, 128), 1) < edge * edge
    low = lax.broadcasted_iota(jnp.int32, (TILES_DEV, 128), 1) < edge * edge

    def unpacked(k, m):
        parts = [recv_s[k, 4 * m + t] for t in range(4)]
        if nch % 2 == 0:
            tail = recv_s[k, 4 * nch + m // 2]
            if m % 2:
                tail = pltpu.roll(tail, 64, 1)
        else:
            tail = recv_s[k, 4 * nch + m]
        parts.append(tail)
        values = []
        for c in range(6):
            first, off = divmod(c * PSLOT, 128)
            value = parts[first]
            if off:
                value = pltpu.roll(value, 128 - off, 1)
                if off + PSLOT > 128:
                    other = pltpu.roll(parts[first + 1], 128 - off, 1)
                    value = jnp.where(lanes8 < 128 - off, value, other)
            values.append(value)
        return values

    def features_of(y, z):
        level = -2.0 * LOG_ROOT - HALF_LOG * (y * y + z * z)
        features = []
        for value in (level, (2.0 * HALF_LOG) * y, (2.0 * HALF_LOG) * z):
            top = value.astype(BF16).astype(F32)
            rest = value - top
            middle = rest.astype(BF16).astype(F32)
            features += [top, middle, rest - middle]
        features.append(jnp.ones((8, 128), F32))
        features = jnp.concatenate(features, axis=0).astype(BF16)
        return jnp.swapaxes(features, 0, 1)[0:PSLOT]

    def left_of(m, r):
        row = [comp_s[m, c, r : r + 1, :] for c in range(4)]
        gap = row[3] - centre
        wx = jnp.exp2(-LOG_ROOT - HALF_LOG * (gap * gap))
        return [row[c] * wx for c in range(3)]

    def arrived(phase, i):
        k = phase * h + lax.rem(i + dest_blk, h)
        pltpu.make_async_copy(recv_s.at[k], recv_s.at[k], recv_sem.at[k]).wait()
        pltpu.make_async_copy(ids_recv_s.at[k], ids_recv_s.at[k], ids_recv_sem.at[k]).wait()

    def take(phase, i):
        k = phase * h + lax.rem(i + dest_blk, h)
        for m in range(nch):
            values = unpacked(k, m)
            for c in range(4):
                comp_s[m, c] = values[c]
            feature_s[m * PSLOT : (m + 1) * PSLOT, :] = features_of(values[4], values[5])

    def weigh():
        exponent = jnp.dot(feature_s[...], basis_ref[...], preferred_element_type=F32)
        for m in range(nch):
            for half in range(2):
                lanes = slice(half * 256, (half + 1) * 256)
                right = jnp.exp2(exponent[m * PSLOT : (m + 1) * PSLOT, lanes])
                right_hi = right.astype(BF16)
                right_s[2 * m + half, 0:PSLOT, :] = right_hi
                right_s[2 * m + half, 128 : 128 + PSLOT, :] = (
                    right - right_hi.astype(F32)
                ).astype(BF16)
                left = []
                for r in range(4 * half, 4 * half + 4):
                    left += left_of(m, r)
                left = jnp.concatenate(left, axis=0)
                left_hi = left.astype(BF16)
                left_s[2 * m + half, 0 : 4 * rows_ci, :] = left_hi
                left_s[2 * m + half, 4 * rows_ci : 8 * rows_ci, :] = (
                    left - left_hi.astype(F32)
                ).astype(BF16)

    def spread(i):
        b = lax.rem(i, batch)
        for u in range(2 * nch):
            left_hi = left_s[u, 0 : 4 * rows_ci, :]
            left_lo = left_s[u, 4 * rows_ci : 8 * rows_ci, :]
            left = jnp.concatenate(
                [
                    jnp.concatenate([left_hi, left_hi], axis=1),
                    jnp.concatenate([left_lo, jnp.zeros_like(left_lo)], axis=1),
                ],
                axis=0,
            )
            both = jnp.dot(left, right_s[u], preferred_element_type=F32)
            for t in range(2):
                lanes = slice(t * 128, (t + 1) * 128)
                at = 2 * t * rows_ci
                even = both[at : at + rows_ci, lanes]
                even = even + both[at + 4 * rows_ci : at + 5 * rows_ci, lanes]
                odd = both[at + rows_ci : at + 2 * rows_ci, lanes]
                odd = odd + both[at + 5 * rows_ci : at + 6 * rows_ci, lanes]
                to = pl.multiple_of((b * pairs + 2 * u + t) * rows_ci, 8)
                share_s[pl.ds(to, rows_ci), :] = jnp.where(low_share, even, odd)

    def gather_tiles(phase, i):
        count = batch * pairs
        names = jnp.zeros((1, 128), jnp.int32)
        for b in range(batch):
            k = phase * h + lax.rem(i - (batch - 1) + b + dest_blk, h)
            row = ids_recv_s[k]
            names = names + (pltpu.roll(row, b * pairs, 1) if b else row)
        tile_of = lax.broadcasted_iota(jnp.int32, (TILES_DEV, 128), 0)
        hot_tile = jnp.concatenate(
            [
                jnp.where(tile_of == names, 1.0, 0.0)[:, 0:count],
                jnp.where(tile_of == pltpu.roll(names, 64, 1), 1.0, 0.0)[:, 0:count],
            ],
            axis=0,
        ).astype(BF16)
        for r in range(rows_ci):
            share = share_s[pl.ds(r, count, stride=rows_ci), :]
            share_hi = share.astype(BF16)
            share_lo = (share - share_hi.astype(F32)).astype(BF16)
            gained = jnp.dot(hot_tile, share_hi, preferred_element_type=F32)
            gained = gained + jnp.dot(hot_tile, share_lo, preferred_element_type=F32)
            total_s[r] = total_s[r] + jnp.where(low, gained[0:TILES_DEV], gained[TILES_DEV:])

    def receive(phase):
        total_s[...] = jnp.zeros_like(total_s)
        arrived(phase, 0)
        take(phase, 0)
        arrived(phase, 1)
        weigh()
        take(phase, 1)

        def step(i, carry):
            arrived(phase, i)
            spread(i - 2)
            weigh()
            take(phase, i)

            @pl.when(lax.rem(i - 2, batch) == batch - 1)
            def _():
                gather_tiles(phase, i - 2)

            return carry

        lax.fori_loop(2, h, step, 0)
        spread(h - 2)
        weigh()
        spread(h - 1)
        gather_tiles(phase, h - 1)

    def folded(c, i):
        even = total_s[c * edge + i]
        odd = total_s[c * edge + i + 1]
        even = even + pltpu.roll(even, 64, 1)
        odd = odd + pltpu.roll(odd, 64, 1)
        return jnp.where(low, even, odd)

    far = pltpu.make_async_remote_copy(
        src_ref=far_s,
        dst_ref=far_recv_s,
        send_sem=far_send_sem,
        recv_sem=far_recv_sem,
        device_id=mirror,
        device_id_type=MESH,
    )
    right_s[...] = jnp.zeros_like(right_s)
    receive(0)
    for c in range(3):
        for i in range(0, edge, 2):
            far_s[c, :, i * 64 : i * 64 + 128] = folded(c, i)
    far.start()
    velocities()
    receive(1)
    far.wait()
    for c in range(3):
        for i in range(0, edge, 2):
            cells = slice(i * 64, i * 64 + 128)
            grid_ref[c, :, cells] = folded(c, i) + far_recv_s[c, :, cells]

    for phase in range(2):
        rest = send_s.at[pl.ds(phase * h + 1, h - 1)]
        pltpu.make_async_copy(rest, rest, send_sem.at[phase]).wait()
        rest_ids = ids_s.at[pl.ds(phase * h + 1, h - 1)]
        pltpu.make_async_copy(rest_ids, rest_ids, ids_send_sem.at[phase]).wait()


def body(
    blob_force, blob_offset, patch_anchor, patch_count, block_owner, block_tile, body_mobility
):
    edge = TILE_EDGE
    lp = blob_force.shape[1]
    group = body_mobility.shape[2]
    length = group * PSLOT
    bodies = lax.axis_size("body")
    bricks = lax.axis_size("brick")
    n = bodies * bricks
    capacity = max(2, 2 * group // n)
    slots = -(-lp * capacity // 8) * 8
    nch = slots // 8
    tiles = 4 * nch + (nch // 2 if nch % 2 == 0 else nch)
    blocks = lp * group
    width = 768
    rpad = -(-4 * lp // 8) * 8
    batch = max(1, 128 // slots)
    while (n // 2) % batch:
        batch //= 2
    dims = (bodies, bricks, lp, group, width, slots, tiles)
    vmem = pl.BlockSpec(memory_space=pltpu.VMEM)
    velocity, grid = pl.pallas_call(
        functools.partial(step_kernel, dims),
        name="step",
        out_shape=(
            jax.ShapeDtypeStruct((3, lp, length), F32),
            jax.ShapeDtypeStruct((3, TILES_DEV, edge**3), F32),
        ),
        in_specs=[vmem] * 8,
        out_specs=(vmem, vmem),
        scratch_shapes=[
            pltpu.VMEM((rpad, group), F32),
            pltpu.VMEM((2, blocks), jnp.int32),
            pltpu.VMEM((lp, length), F32),
            pltpu.VMEM((6, lp, width), F32),
            pltpu.VMEM((lp, 8, 640), F32),
            pltpu.VMEM((lp, group, 640), F32),
            pltpu.VMEM((3, blocks, 640), BF16),
            pltpu.VMEM((n, tiles, 8, 128), F32),
            pltpu.VMEM((n, 1, 128), jnp.int32),
            pltpu.VMEM((n, tiles, 8, 128), F32),
            pltpu.VMEM((n, 1, 128), jnp.int32),
            pltpu.VMEM((nch, 4, 8, 128), F32),
            pltpu.VMEM((nch * PSLOT, 80), BF16),
            pltpu.VMEM((2 * nch, 256, 4 * edge * edge), BF16),
            pltpu.VMEM((2 * nch, 24 * edge, 128), BF16),
            pltpu.VMEM((batch * slots // 2 * 3 * edge, 128), F32),
            pltpu.VMEM((3 * edge, TILES_DEV, 128), F32),
            pltpu.VMEM((8, group), F32),
            pltpu.VMEM((bricks, 8, group), F32),
            pltpu.VMEM((3, TILES_DEV, edge**3), F32),
            pltpu.VMEM((3, TILES_DEV, edge**3), F32),
            pltpu.SemaphoreType.DMA((2,)),
            pltpu.SemaphoreType.DMA((n,)),
            pltpu.SemaphoreType.DMA((2,)),
            pltpu.SemaphoreType.DMA((n,)),
            pltpu.SemaphoreType.DMA((bricks,)),
            pltpu.SemaphoreType.DMA((bricks,)),
            pltpu.SemaphoreType.DMA,
            pltpu.SemaphoreType.DMA,
        ],
        compiler_params=pltpu.CompilerParams(
            collective_id=0, has_side_effects=True, vmem_limit_bytes=60 << 20
        ),
    )(
        blob_force,
        blob_offset,
        patch_anchor,
        jnp.transpose(patch_count),
        jnp.transpose(block_owner, (0, 2, 1)),
        block_tile,
        body_mobility,
        jnp.asarray(exponent_basis(edge)),
    )
    return velocity, jnp.transpose(grid, (1, 0, 2))


def solution(mesh):
    in_specs = (
        P(None, "brick", "body"),
        P(None, "brick", "body"),
        P(None, "brick", "body"),
        P("body", "brick"),
        P("brick", "body", None),
        P("brick", "body"),
        P(None, None, "body"),
    )
    out_specs = (P(None, "brick", "body"), P(("body", "brick"), None, None))
    return jax.shard_map(body, mesh=mesh, in_specs=in_specs, out_specs=out_specs, check_vma=False)
```

```python
import functools
import math

import jax
import jax.numpy as jnp
import ml_dtypes
import numpy as np
from jax import lax
from jax.experimental import pallas as pl
from jax.experimental.pallas import tpu as pltpu
from jax.sharding import PartitionSpec as P

PSLOT = 96
TILE_EDGE = 8
TILES_DEV = 32
LOG_ROOT = 0.5 * math.log2(2.0 * math.pi)
HALF_LOG = 0.5 / math.log(2.0)
MESH = pl.DeviceIdType.MESH
NT = (((1,), (1,)), ((), ()))
F32 = jnp.float32
BF16 = jnp.bfloat16


def stack3(x):
    hi = x.astype(BF16).astype(F32)
    rest = x - hi
    mid = rest.astype(BF16).astype(F32)
    lo = rest - mid
    return jnp.concatenate([hi, mid, lo], axis=0).astype(BF16)


def cross(left, right):
    return (
        left[1] * right[2] - left[2] * right[1],
        left[2] * right[0] - left[0] * right[2],
        left[0] * right[1] - left[1] * right[0],
    )


def segment_matrix(group, width, base):
    lane = lax.broadcasted_iota(jnp.int32, (group, width), 1) + base
    start = lax.broadcasted_iota(jnp.int32, (group, width), 0) * PSLOT
    gap = lane - start
    return jnp.where((gap >= 0) & (gap < PSLOT), 1.0, 0.0).astype(BF16)


def exponent_basis(edge):
    cells = edge * edge
    centre = np.arange(edge, dtype=np.float32) + 0.5 - edge / 2
    first = np.repeat(centre, edge)
    second = np.tile(centre, edge)
    basis = np.zeros((80, 8, cells), np.float32)
    for slot in range(8):
        for part in range(3):
            basis[8 * part + slot, slot] = 1.0
            basis[24 + 8 * part + slot, slot] = first
            basis[48 + 8 * part + slot, slot] = second
    rest = (-HALF_LOG * (first**2 + second**2)).astype(np.float32)
    for part in range(3):
        top = rest.astype(ml_dtypes.bfloat16).astype(np.float32)
        basis[72 + part, :] = top
        rest = rest - top
    return basis.reshape(80, 8 * cells).astype(ml_dtypes.bfloat16)


def step_kernel(
    dims,
    force_hbm,
    offset_hbm,
    anchor_hbm,
    count_hbm,
    owner_hbm,
    tile_hbm,
    mob_hbm,
    basis_hbm,
    vel_ref,
    grid_ref,
    rows_s,
    meta_s,
    live_s,
    flat_s,
    turn_s,
    data_s,
    split_s,
    send_s,
    ids_s,
    recv_s,
    ids_recv_s,
    comp_s,
    feature_s,
    right_s,
    left_s,
    share_s,
    total_s,
    wr_s,
    wrecv_s,
    far_s,
    far_recv_s,
    send_sem,
    recv_sem,
    ids_send_sem,
    ids_recv_sem,
    wr_send_sem,
    wr_recv_sem,
    far_send_sem,
    far_recv_sem,
    force_ref,
    offset_ref,
    anchor_ref,
    count_ref,
    owner_ref,
    tile_ref,
    mob_ref,
    basis_ref,
    in_sem,
):
    bodies, bricks, lp, group, width, slots, tiles = dims
    n = bodies * bricks
    h = n // 2
    turn = h // 2 if h % 2 == 0 else 0
    length = group * PSLOT
    chunks = length // width
    per = width // PSLOT
    rpad = rows_s.shape[0]
    blocks = lp * group
    my_body = lax.axis_index("body")
    my_brick = lax.axis_index("brick")
    me = my_body * bricks + my_brick
    my_half = me // h
    mine = lax.rem(me, h)

    def device(half, place):
        d = half * h + place
        return (d // bricks, lax.rem(d, bricks))

    mirror = device(1 - my_half, lax.rem(mine + turn, h))

    loads = [
        pltpu.make_async_copy(source, target, in_sem.at[i])
        for i, (source, target) in enumerate(
            (
                (anchor_hbm, anchor_ref),
                (count_hbm, count_ref),
                (owner_hbm, owner_ref),
                (tile_hbm, tile_ref),
                (force_hbm, force_ref),
                (offset_hbm, offset_ref),
                (mob_hbm, mob_ref),
                (basis_hbm, basis_ref),
            )
        )
    ]
    for load in loads:
        load.start()

    barrier = pltpu.get_barrier_semaphore()

    def greet(k, carry):
        pl.semaphore_signal(
            barrier,
            inc=1,
            device_id=device(my_half, lax.rem(mine + k, h)),
            device_id_type=MESH,
        )
        return carry

    pl.semaphore_signal(barrier, inc=1, device_id=mirror, device_id_type=MESH)
    lax.fori_loop(1, h, greet, 0)

    for load in loads:
        load.wait()
    rows_s[...] = jnp.zeros_like(rows_s)
    for c in range(3):
        rows_s[c * lp : (c + 1) * lp, :] = anchor_ref[c] - TILE_EDGE / 2
    starts = PSLOT * lax.broadcasted_iota(jnp.int32, (lp, group), 1)
    rows_s[3 * lp : 4 * lp, :] = (count_ref[...] + starts).astype(F32)
    for q in range(lp):
        meta_s[0:1, q * group : (q + 1) * group] = owner_ref[q]
        meta_s[1:2, q * group : (q + 1) * group] = tile_ref[q : q + 1, :]
    rows3 = stack3(rows_s[...])

    def chunk(j, carry):
        base = pl.multiple_of(j * width, 128)
        seg = segment_matrix(group, width, base)
        flat3 = jnp.dot(rows3, seg, preferred_element_type=F32)
        flat = flat3[0:rpad] + flat3[rpad : 2 * rpad] + flat3[2 * rpad : 3 * rpad]
        lane = (lax.broadcasted_iota(jnp.int32, (lp, width), 1) + base).astype(F32)
        live = jnp.where(lane < flat[3 * lp : 4 * lp], 1.0, 0.0)
        live_s[:, pl.ds(base, width)] = live
        loaded = [force_ref[c, :, pl.ds(base, width)] * live for c in range(3)]
        offset = [offset_ref[c, :, pl.ds(base, width)] for c in range(3)]
        for c in range(3):
            flat_s[c] = loaded[c]
            flat_s[3 + c] = offset[c] + flat[c * lp : (c + 1) * lp]
        for m in range(per):
            for c in range(6):
                piece = flat_s[c, :, m * PSLOT : (m + 1) * PSLOT]
                for q in range(lp):
                    turn_s[q, m : m + 1, c * PSLOT : (c + 1) * PSLOT] = piece[q : q + 1]
        data_s[:, pl.ds(pl.multiple_of(j * per, per), per), :] = turn_s[...]
        return carry

    lax.fori_loop(0, chunks, chunk, 0, unroll=8)

    data = data_s[...].reshape(blocks, 640)
    tail = data[:, 512:576]
    data = jnp.concatenate([data[:, 0:512], tail, tail], axis=1)
    data_hi = data.astype(BF16)
    split_s[0] = data_hi
    split_s[1] = (data - data_hi.astype(F32)).astype(BF16)

    owner = meta_s[0:1, :]
    tile = meta_s[1:2, :]
    place = lax.rem(owner, h)
    proxy = place + turn
    proxy = jnp.where(proxy >= h, proxy - h, proxy)
    owner = jnp.where(owner // h == my_half, place + h, proxy)
    is_owner = lax.broadcasted_iota(jnp.int32, (n, blocks), 0) == owner
    hot = jnp.where(is_owner, 1.0, 0.0)
    before = jnp.where(
        lax.broadcasted_iota(jnp.int32, (blocks, blocks), 0)
        < lax.broadcasted_iota(jnp.int32, (blocks, blocks), 1),
        1.0,
        0.0,
    ).astype(BF16)
    seen = jnp.dot(hot.astype(BF16), before, preferred_element_type=F32)
    rank = jnp.sum(hot * seen, axis=0, keepdims=True)
    rank = (rank + 0.5).astype(jnp.int32)
    lane_of = rank // 2 + 64 * lax.rem(rank, 2)
    rank_hot = jnp.where(
        lax.broadcasted_iota(jnp.int32, (128, blocks), 0) == lane_of, 1.0, 0.0
    ).astype(BF16)
    weighted = (hot * tile.astype(F32)).astype(BF16)
    ids = lax.dot_general(weighted, rank_hot, NT, preferred_element_type=F32)
    ids_s[:, 0, :] = (ids + 0.5).astype(jnp.int32)
    slot_of = owner * slots + rank

    dest_blk = max(1, 128 // slots)
    while h % dest_blk:
        dest_blk //= 2
    rows = dest_blk * slots
    planes = h // dest_blk
    my_plane = mine // dest_blk
    my_place = lax.rem(mine, dest_blk)

    def plane_of(g):
        if planes & (planes - 1):
            return lax.rem(my_plane + g, planes)
        total = jnp.int32(0)
        bit = 1
        while bit < planes:
            total = total + lax.rem(my_plane // bit + g // bit, 2) * bit
            bit *= 2
        return total

    def dest_of(g, j):
        return plane_of(g) * dest_blk + lax.rem(my_place + j, dest_blk)


    pl.semaphore_wait(barrier, h)

    def wr_copy(k):
        other = lax.rem(my_brick + k, bricks)
        return pltpu.make_async_remote_copy(
            src_ref=wr_s,
            dst_ref=wrecv_s.at[my_brick],
            send_sem=wr_send_sem.at[k],
            recv_sem=wr_recv_sem.at[k],
            device_id=(my_body, other),
            device_id_type=MESH,
        )

    def start(phase, k, carry):
        d = dest_of(k // dest_blk, lax.rem(k, dest_blk))
        where = device(my_half, d)
        slot = phase * h + k
        pltpu.make_async_remote_copy(
            src_ref=send_s.at[slot],
            dst_ref=recv_s.at[slot],
            send_sem=send_sem.at[phase],
            recv_sem=recv_sem.at[slot],
            device_id=where,
            device_id_type=MESH,
        ).start()
        pltpu.make_async_remote_copy(
            src_ref=ids_s.at[phase * h + d],
            dst_ref=ids_recv_s.at[slot],
            send_sem=ids_send_sem.at[phase],
            recv_sem=ids_recv_sem.at[slot],
            device_id=where,
            device_id_type=MESH,
        ).start()
        return carry

    def pack(i, carry):
        phase = i // planes
        g = lax.rem(i + 1, planes)
        place = lax.broadcasted_iota(jnp.int32, (rows, blocks), 0) + my_place * slots
        place = jnp.where(place >= rows, place - rows, place)
        target = phase * (h * slots) + plane_of(g) * rows + place
        pick = jnp.where(target == slot_of, 1.0, 0.0).astype(BF16)
        out = jnp.dot(pick, split_s[0], preferred_element_type=F32)
        out = out + jnp.dot(pick, split_s[1], preferred_element_type=F32)
        low = lax.broadcasted_iota(jnp.int32, (8, 128), 1) < 64
        nch = slots // 8
        for d in range(dest_blk):
            k = phase * h + g * dest_blk + d
            for m in range(nch):
                r = d * slots + m * 8
                for t in range(4):
                    send_s[k, m * 4 + t] = out[r : r + 8, t * 128 : (t + 1) * 128]
            if nch % 2 == 0:
                for m in range(0, nch, 2):
                    r = d * slots + m * 8
                    send_s[k, 4 * nch + m // 2] = jnp.where(
                        low, out[r : r + 8, 512:640], out[r + 8 : r + 16, 512:640]
                    )
            else:
                for m in range(nch):
                    r = d * slots + m * 8
                    send_s[k, 4 * nch + m] = out[r : r + 8, 512:640]

        least = jnp.where(g == 0, 1, 0)
        lax.fori_loop(
            g * dest_blk + least, (g + 1) * dest_blk, functools.partial(start, phase), 0
        )
        return carry

    def own_copies(phase):
        k = phase * h
        return (
            pltpu.make_async_copy(send_s.at[k], recv_s.at[k], recv_sem.at[k]),
            pltpu.make_async_copy(ids_s.at[k + mine], ids_recv_s.at[k], ids_recv_sem.at[k]),
        )

    lax.fori_loop(0, 2 * planes, pack, 0)
    for phase in range(2):
        for copy in own_copies(phase):
            copy.start()

    def wrench_part(j, wrench):
        base = pl.multiple_of(j * width, 128)
        seg = segment_matrix(group, width, base)
        live = live_s[:, pl.ds(base, width)]
        loaded = [force_ref[c, :, pl.ds(base, width)] * live for c in range(3)]
        offset = [offset_ref[c, :, pl.ds(base, width)] for c in range(3)]
        torque = cross(offset, loaded)
        sums = [jnp.sum(v, axis=0, keepdims=True) for v in loaded + list(torque)]
        sums = jnp.concatenate(sums + [jnp.zeros((2, width), F32)], axis=0)
        return wrench + lax.dot_general(stack3(sums), seg, NT, preferred_element_type=F32)

    wrench3 = lax.fori_loop(0, chunks, wrench_part, jnp.zeros((24, group), F32), unroll=8)
    wr_s[...] = wrench3[0:8] + wrench3[8:16] + wrench3[16:24]
    wrecv_s[my_brick] = wr_s[...]
    for k in range(1, bricks):
        wr_copy(k).start()

    def velocities():
        for k in range(1, bricks):
            wr_copy(k).wait()
        wrench = wrecv_s[0]
        for k in range(1, bricks):
            wrench = wrench + wrecv_s[k]
        velocity = [jnp.sum(mob_ref[i] * wrench[0:6], axis=0, keepdims=True) for i in range(6)]
        velocity = jnp.concatenate(velocity + [jnp.zeros((2, group), F32)], axis=0)
        vel3 = stack3(velocity)

        def spread_velocity(j, carry):
            base = pl.multiple_of(j * width, 128)
            seg = segment_matrix(group, width, base)
            v3 = jnp.dot(vel3, seg, preferred_element_type=F32)
            v = v3[0:8] + v3[8:16] + v3[16:24]
            live = live_s[:, pl.ds(base, width)]
            offset = [offset_ref[c, :, pl.ds(base, width)] for c in range(3)]
            spin = cross([v[3:4], v[4:5], v[5:6]], offset)
            for c in range(3):
                vel_ref[c, :, pl.ds(base, width)] = (v[c : c + 1] + spin[c]) * live
            return carry

        lax.fori_loop(0, chunks, spread_velocity, 0, unroll=8)

    nch = slots // 8
    edge = TILE_EDGE
    rows_ci = 3 * edge
    batch = dest_blk
    lanes8 = lax.broadcasted_iota(jnp.int32, (8, 128), 1)
    centre = lax.broadcasted_iota(jnp.int32, (edge, 128), 0).astype(F32) + (0.5 - edge / 2)
    pairs = slots // 2
    low_share = lax.broadcasted_iota(jnp.int32, (rows_ci, 128), 1) < edge * edge
    low = lax.broadcasted_iota(jnp.int32, (TILES_DEV, 128), 1) < edge * edge

    def unpacked(k, m):
        parts = [recv_s[k, 4 * m + t] for t in range(4)]
        if nch % 2 == 0:
            tail = recv_s[k, 4 * nch + m // 2]
            if m % 2:
                tail = pltpu.roll(tail, 64, 1)
        else:
            tail = recv_s[k, 4 * nch + m]
        parts.append(tail)
        values = []
        for c in range(6):
            first, off = divmod(c * PSLOT, 128)
            value = parts[first]
            if off:
                value = pltpu.roll(value, 128 - off, 1)
                if off + PSLOT > 128:
                    other = pltpu.roll(parts[first + 1], 128 - off, 1)
                    value = jnp.where(lanes8 < 128 - off, value, other)
            values.append(value)
        return values

    def features_of(y, z):
        level = -2.0 * LOG_ROOT - HALF_LOG * (y * y + z * z)
        features = []
        for value in (level, (2.0 * HALF_LOG) * y, (2.0 * HALF_LOG) * z):
            top = value.astype(BF16).astype(F32)
            rest = value - top
            middle = rest.astype(BF16).astype(F32)
            features += [top, middle, rest - middle]
        features.append(jnp.ones((8, 128), F32))
        features = jnp.concatenate(features, axis=0).astype(BF16)
        return jnp.swapaxes(features, 0, 1)[0:PSLOT]

    def left_of(m, r):
        row = [comp_s[m, c, r : r + 1, :] for c in range(4)]
        gap = row[3] - centre
        wx = jnp.exp2(-LOG_ROOT - HALF_LOG * (gap * gap))
        return [row[c] * wx for c in range(3)]

    def nth(i):
        other = jnp.where(i > h - dest_blk, i - (h - dest_blk), i - 1 + dest_blk)
        return jnp.where(i == 0, 0, other)

    def arrived(phase, i):
        k = phase * h + nth(i)
        pltpu.make_async_copy(recv_s.at[k], recv_s.at[k], recv_sem.at[k]).wait()
        pltpu.make_async_copy(ids_recv_s.at[k], ids_recv_s.at[k], ids_recv_sem.at[k]).wait()

    def take(phase, i):
        k = phase * h + nth(i)
        for m in range(nch):
            values = unpacked(k, m)
            for c in range(4):
                comp_s[m, c] = values[c]
            feature_s[m * PSLOT : (m + 1) * PSLOT, :] = features_of(values[4], values[5])

    def weigh():
        exponent = jnp.dot(feature_s[...], basis_ref[...], preferred_element_type=F32)
        for m in range(nch):
            for half in range(2):
                lanes = slice(half * 256, (half + 1) * 256)
                right = jnp.exp2(exponent[m * PSLOT : (m + 1) * PSLOT, lanes])
                right_hi = right.astype(BF16)
                right_s[2 * m + half, 0:PSLOT, :] = right_hi
                right_s[2 * m + half, 128 : 128 + PSLOT, :] = (
                    right - right_hi.astype(F32)
                ).astype(BF16)
                left = []
                for r in range(4 * half, 4 * half + 4):
                    left += left_of(m, r)
                left = jnp.concatenate(left, axis=0)
                left_hi = left.astype(BF16)
                left_s[2 * m + half, 0 : 4 * rows_ci, :] = left_hi
                left_s[2 * m + half, 4 * rows_ci : 8 * rows_ci, :] = (
                    left - left_hi.astype(F32)
                ).astype(BF16)

    def spread(i):
        b = lax.rem(i, batch)
        for u in range(2 * nch):
            left_hi = left_s[u, 0 : 4 * rows_ci, :]
            left_lo = left_s[u, 4 * rows_ci : 8 * rows_ci, :]
            left = jnp.concatenate(
                [
                    jnp.concatenate([left_hi, left_hi], axis=1),
                    jnp.concatenate([left_lo, jnp.zeros_like(left_lo)], axis=1),
                ],
                axis=0,
            )
            both = jnp.dot(left, right_s[u], preferred_element_type=F32)
            for t in range(2):
                lanes = slice(t * 128, (t + 1) * 128)
                at = 2 * t * rows_ci
                even = both[at : at + rows_ci, lanes]
                even = even + both[at + 4 * rows_ci : at + 5 * rows_ci, lanes]
                odd = both[at + rows_ci : at + 2 * rows_ci, lanes]
                odd = odd + both[at + 5 * rows_ci : at + 6 * rows_ci, lanes]
                to = pl.multiple_of((b * pairs + 2 * u + t) * rows_ci, 8)
                share_s[pl.ds(to, rows_ci), :] = jnp.where(low_share, even, odd)

    def gather_tiles(phase, i, finish=None):
        count = batch * pairs
        names = jnp.zeros((1, 128), jnp.int32)
        for b in range(batch):
            k = phase * h + nth(i - (batch - 1) + b)
            row = ids_recv_s[k]
            names = names + (pltpu.roll(row, b * pairs, 1) if b else row)
        tile_of = lax.broadcasted_iota(jnp.int32, (TILES_DEV, 128), 0)
        hot_tile = jnp.concatenate(
            [
                jnp.where(tile_of == names, 1.0, 0.0)[:, 0:count],
                jnp.where(tile_of == pltpu.roll(names, 64, 1), 1.0, 0.0)[:, 0:count],
            ],
            axis=0,
        ).astype(BF16)
        for r in range(rows_ci):
            share = share_s[pl.ds(r, count, stride=rows_ci), :]
            share_hi = share.astype(BF16)
            share_lo = (share - share_hi.astype(F32)).astype(BF16)
            gained = jnp.dot(hot_tile, share_hi, preferred_element_type=F32)
            gained = gained + jnp.dot(hot_tile, share_lo, preferred_element_type=F32)
            total_s[r] = total_s[r] + jnp.where(low, gained[0:TILES_DEV], gained[TILES_DEV:])
            if finish is not None and r % edge == edge - 1:
                finish(r // edge)

    def receive(phase, finish):
        total_s[...] = jnp.zeros_like(total_s)
        arrived(phase, 0)
        take(phase, 0)
        arrived(phase, 1)
        weigh()
        take(phase, 1)

        def step(i, carry):
            arrived(phase, i)
            spread(i - 2)
            weigh()
            take(phase, i)

            @pl.when(lax.rem(i - 2, batch) == batch - 1)
            def _():
                gather_tiles(phase, i - 2)

            return carry

        lax.fori_loop(2, h, step, 0)
        spread(h - 2)
        weigh()
        spread(h - 1)
        gather_tiles(phase, h - 1, finish)

    def folded(c, i):
        even = total_s[c * edge + i]
        odd = total_s[c * edge + i + 1]
        even = even + pltpu.roll(even, 64, 1)
        odd = odd + pltpu.roll(odd, 64, 1)
        return jnp.where(low, even, odd)

    def far_copy(c):
        return pltpu.make_async_remote_copy(
            src_ref=far_s.at[c],
            dst_ref=far_recv_s.at[c],
            send_sem=far_send_sem.at[c],
            recv_sem=far_recv_sem.at[c],
            device_id=mirror,
            device_id_type=MESH,
        )

    def send_far(c):
        for i in range(0, edge, 2):
            far_s[c, :, i * 64 : i * 64 + 128] = folded(c, i)
        far_copy(c).start()

    def write_grid(c):
        for i in range(0, edge, 2):
            grid_ref[c, :, i * 64 : i * 64 + 128] = folded(c, i)

    right_s[...] = jnp.zeros_like(right_s)
    receive(0, send_far)
    velocities()
    receive(1, write_grid)
    for c in range(3):
        far_copy(c).wait()
        grid_ref[c] = grid_ref[c] + far_recv_s[c]

    for phase in range(2):
        rest = send_s.at[pl.ds(phase * h + 1, h - 1)]
        pltpu.make_async_copy(rest, rest, send_sem.at[phase]).wait()
        rest_ids = ids_s.at[pl.ds(phase * h + 1, h - 1)]
        pltpu.make_async_copy(rest_ids, rest_ids, ids_send_sem.at[phase]).wait()


def body(
    blob_force, blob_offset, patch_anchor, patch_count, block_owner, block_tile, body_mobility
):
    edge = TILE_EDGE
    lp = blob_force.shape[1]
    group = body_mobility.shape[2]
    length = group * PSLOT
    bodies = lax.axis_size("body")
    bricks = lax.axis_size("brick")
    n = bodies * bricks
    capacity = max(2, 2 * group // n)
    slots = -(-lp * capacity // 8) * 8
    nch = slots // 8
    tiles = 4 * nch + (nch // 2 if nch % 2 == 0 else nch)
    blocks = lp * group
    width = 768
    rpad = -(-4 * lp // 8) * 8
    batch = max(1, 128 // slots)
    while (n // 2) % batch:
        batch //= 2
    dims = (bodies, bricks, lp, group, width, slots, tiles)
    limit = (16 << 20) + 2 * n * (tiles + 1) * 4096
    vmem = pl.BlockSpec(memory_space=pltpu.VMEM)
    velocity, grid = pl.pallas_call(
        functools.partial(step_kernel, dims),
        name="step",
        out_shape=(
            jax.ShapeDtypeStruct((3, lp, length), F32),
            jax.ShapeDtypeStruct((3, TILES_DEV, edge**3), F32),
        ),
        in_specs=[pl.BlockSpec(memory_space=pltpu.HBM)] * 8,
        out_specs=(vmem, vmem),
        scratch_shapes=[
            pltpu.VMEM((rpad, group), F32),
            pltpu.VMEM((2, blocks), jnp.int32),
            pltpu.VMEM((lp, length), F32),
            pltpu.VMEM((6, lp, width), F32),
            pltpu.VMEM((lp, 8, 640), F32),
            pltpu.VMEM((lp, group, 640), F32),
            pltpu.VMEM((2, blocks, 640), BF16),
            pltpu.VMEM((n, tiles, 8, 128), F32),
            pltpu.VMEM((n, 1, 128), jnp.int32),
            pltpu.VMEM((n, tiles, 8, 128), F32),
            pltpu.VMEM((n, 1, 128), jnp.int32),
            pltpu.VMEM((nch, 4, 8, 128), F32),
            pltpu.VMEM((nch * PSLOT, 80), BF16),
            pltpu.VMEM((2 * nch, 256, 4 * edge * edge), BF16),
            pltpu.VMEM((2 * nch, 24 * edge, 128), BF16),
            pltpu.VMEM((batch * slots // 2 * 3 * edge, 128), F32),
            pltpu.VMEM((3 * edge, TILES_DEV, 128), F32),
            pltpu.VMEM((8, group), F32),
            pltpu.VMEM((bricks, 8, group), F32),
            pltpu.VMEM((3, TILES_DEV, edge**3), F32),
            pltpu.VMEM((3, TILES_DEV, edge**3), F32),
            pltpu.SemaphoreType.DMA((2,)),
            pltpu.SemaphoreType.DMA((n,)),
            pltpu.SemaphoreType.DMA((2,)),
            pltpu.SemaphoreType.DMA((n,)),
            pltpu.SemaphoreType.DMA((bricks,)),
            pltpu.SemaphoreType.DMA((bricks,)),
            pltpu.SemaphoreType.DMA((3,)),
            pltpu.SemaphoreType.DMA((3,)),
            pltpu.VMEM((3, lp, length), F32),
            pltpu.VMEM((3, lp, length), F32),
            pltpu.VMEM((3, lp, group), F32),
            pltpu.VMEM((lp, group), jnp.int32),
            pltpu.VMEM((lp, 1, group), jnp.int32),
            pltpu.VMEM((lp, group), jnp.int32),
            pltpu.VMEM((6, 6, group), F32),
            pltpu.VMEM((80, 8 * edge * edge), BF16),
            pltpu.SemaphoreType.DMA((8,)),
        ],
        compiler_params=pltpu.CompilerParams(
            collective_id=0, has_side_effects=True, vmem_limit_bytes=limit
        ),
    )(*[
        pltpu.with_memory_space_constraint(x, pltpu.HBM)
        for x in (
            blob_force,
            blob_offset,
            patch_anchor,
            jnp.transpose(patch_count),
            jnp.transpose(block_owner, (0, 2, 1)),
            block_tile,
            body_mobility,
            jnp.asarray(exponent_basis(edge)),
        )
    ])
    return velocity, jnp.transpose(grid, (1, 0, 2))


def solution(mesh):
    in_specs = (
        P(None, "brick", "body"),
        P(None, "brick", "body"),
        P(None, "brick", "body"),
        P("body", "brick"),
        P("brick", "body", None),
        P("brick", "body"),
        P(None, None, "body"),
    )
    out_specs = (P(None, "brick", "body"), P(("body", "brick"), None, None))
    return jax.shard_map(body, mesh=mesh, in_specs=in_specs, out_specs=out_specs, check_vma=False)
```

```python
import functools
import math

import jax
import jax.numpy as jnp
import ml_dtypes
import numpy as np
from jax import lax
from jax.experimental import pallas as pl
from jax.experimental.pallas import tpu as pltpu
from jax.sharding import PartitionSpec as P

PSLOT = 96
TILE_EDGE = 8
TILES_DEV = 32
LOG_ROOT = 0.5 * math.log2(2.0 * math.pi)
HALF_LOG = 0.5 / math.log(2.0)
MESH = pl.DeviceIdType.MESH
NT = (((1,), (1,)), ((), ()))
F32 = jnp.float32
BF16 = jnp.bfloat16


def stack3(x):
    hi = x.astype(BF16).astype(F32)
    rest = x - hi
    mid = rest.astype(BF16).astype(F32)
    lo = rest - mid
    return jnp.concatenate([hi, mid, lo], axis=0).astype(BF16)


def cross(left, right):
    return (
        left[1] * right[2] - left[2] * right[1],
        left[2] * right[0] - left[0] * right[2],
        left[0] * right[1] - left[1] * right[0],
    )


def segment_matrix(group, width, base):
    lane = lax.broadcasted_iota(jnp.int32, (group, width), 1) + base
    start = lax.broadcasted_iota(jnp.int32, (group, width), 0) * PSLOT
    gap = lane - start
    return jnp.where((gap >= 0) & (gap < PSLOT), 1.0, 0.0).astype(BF16)


def exponent_basis(edge):
    cells = edge * edge
    centre = np.arange(edge, dtype=np.float32) + 0.5 - edge / 2
    first = np.repeat(centre, edge)
    second = np.tile(centre, edge)
    basis = np.zeros((80, 8, cells), np.float32)
    for slot in range(8):
        for part in range(3):
            basis[8 * part + slot, slot] = 1.0
            basis[24 + 8 * part + slot, slot] = first
            basis[48 + 8 * part + slot, slot] = second
    rest = (-HALF_LOG * (first**2 + second**2)).astype(np.float32)
    for part in range(3):
        top = rest.astype(ml_dtypes.bfloat16).astype(np.float32)
        basis[72 + part, :] = top
        rest = rest - top
    return basis.reshape(80, 8 * cells).astype(ml_dtypes.bfloat16)


def step_kernel(
    dims,
    force_hbm,
    offset_hbm,
    anchor_hbm,
    count_hbm,
    owner_hbm,
    tile_hbm,
    mob_hbm,
    basis_hbm,
    vel_ref,
    grid_ref,
    rows_s,
    meta_s,
    live_s,
    flat_s,
    turn_s,
    data_s,
    split_s,
    send_s,
    ids_s,
    recv_s,
    ids_recv_s,
    comp_s,
    feature_s,
    right_s,
    left_s,
    share_s,
    total_s,
    wr_s,
    wrecv_s,
    far_s,
    far_recv_s,
    send_sem,
    recv_sem,
    ids_send_sem,
    ids_recv_sem,
    wr_send_sem,
    wr_recv_sem,
    far_send_sem,
    far_recv_sem,
    force_ref,
    offset_ref,
    anchor_ref,
    count_ref,
    owner_ref,
    tile_ref,
    mob_ref,
    basis_ref,
    in_sem,
):
    bodies, bricks, lp, group, width, slots, tiles = dims
    n = bodies * bricks
    h = n // 2
    turn = h // 2 if h % 2 == 0 else 0
    length = group * PSLOT
    chunks = length // width
    per = width // PSLOT
    rpad = rows_s.shape[0]
    blocks = lp * group
    my_body = lax.axis_index("body")
    my_brick = lax.axis_index("brick")
    me = my_body * bricks + my_brick
    my_half = me // h
    mine = lax.rem(me, h)

    def device(half, place):
        d = half * h + place
        return (d // bricks, lax.rem(d, bricks))

    mirror = device(1 - my_half, lax.rem(mine + turn, h))

    loads = [
        pltpu.make_async_copy(source, target, in_sem.at[i])
        for i, (source, target) in enumerate(
            (
                (anchor_hbm, anchor_ref),
                (count_hbm, count_ref),
                (owner_hbm, owner_ref),
                (tile_hbm, tile_ref),
                (force_hbm, force_ref),
                (offset_hbm, offset_ref),
                (mob_hbm, mob_ref),
                (basis_hbm, basis_ref),
            )
        )
    ]
    for load in loads:
        load.start()

    barrier = pltpu.get_barrier_semaphore()

    def greet(k, carry):
        pl.semaphore_signal(
            barrier,
            inc=1,
            device_id=device(my_half, lax.rem(mine + k, h)),
            device_id_type=MESH,
        )
        return carry

    pl.semaphore_signal(barrier, inc=1, device_id=mirror, device_id_type=MESH)
    lax.fori_loop(1, h, greet, 0)

    for load in loads:
        load.wait()
    rows_s[...] = jnp.zeros_like(rows_s)
    for c in range(3):
        rows_s[c * lp : (c + 1) * lp, :] = anchor_ref[c] - TILE_EDGE / 2
    starts = PSLOT * lax.broadcasted_iota(jnp.int32, (lp, group), 1)
    rows_s[3 * lp : 4 * lp, :] = (count_ref[...] + starts).astype(F32)
    for q in range(lp):
        meta_s[0:1, q * group : (q + 1) * group] = owner_ref[q]
        meta_s[1:2, q * group : (q + 1) * group] = tile_ref[q : q + 1, :]
    rows3 = stack3(rows_s[...])

    def chunk(j, carry):
        base = pl.multiple_of(j * width, 128)
        seg = segment_matrix(group, width, base)
        flat3 = jnp.dot(rows3, seg, preferred_element_type=F32)
        flat = flat3[0:rpad] + flat3[rpad : 2 * rpad] + flat3[2 * rpad : 3 * rpad]
        lane = (lax.broadcasted_iota(jnp.int32, (lp, width), 1) + base).astype(F32)
        live = jnp.where(lane < flat[3 * lp : 4 * lp], 1.0, 0.0)
        live_s[:, pl.ds(base, width)] = live
        loaded = [force_ref[c, :, pl.ds(base, width)] * live for c in range(3)]
        offset = [offset_ref[c, :, pl.ds(base, width)] for c in range(3)]
        for c in range(3):
            flat_s[c] = loaded[c]
            flat_s[3 + c] = offset[c] + flat[c * lp : (c + 1) * lp]
        for m in range(per):
            for c in range(6):
                piece = flat_s[c, :, m * PSLOT : (m + 1) * PSLOT]
                for q in range(lp):
                    turn_s[q, m : m + 1, c * PSLOT : (c + 1) * PSLOT] = piece[q : q + 1]
        data_s[:, pl.ds(pl.multiple_of(j * per, per), per), :] = turn_s[...]
        return carry

    lax.fori_loop(0, chunks, chunk, 0, unroll=8)

    data = data_s[...].reshape(blocks, 640)
    tail = data[:, 512:576]
    data = jnp.concatenate([data[:, 0:512], tail, tail], axis=1)
    data_hi = data.astype(BF16)
    split_s[0] = data_hi
    split_s[1] = (data - data_hi.astype(F32)).astype(BF16)

    owner = meta_s[0:1, :]
    tile = meta_s[1:2, :]
    place = lax.rem(owner, h)
    proxy = place + turn
    proxy = jnp.where(proxy >= h, proxy - h, proxy)
    owner = jnp.where(owner // h == my_half, place + h, proxy)
    is_owner = lax.broadcasted_iota(jnp.int32, (n, blocks), 0) == owner
    hot = jnp.where(is_owner, 1.0, 0.0)
    before = jnp.where(
        lax.broadcasted_iota(jnp.int32, (blocks, blocks), 0)
        < lax.broadcasted_iota(jnp.int32, (blocks, blocks), 1),
        1.0,
        0.0,
    ).astype(BF16)
    seen = jnp.dot(hot.astype(BF16), before, preferred_element_type=F32)
    rank = jnp.sum(hot * seen, axis=0, keepdims=True)
    rank = (rank + 0.5).astype(jnp.int32)
    lane_of = rank // 2 + 64 * lax.rem(rank, 2)
    rank_hot = jnp.where(
        lax.broadcasted_iota(jnp.int32, (128, blocks), 0) == lane_of, 1.0, 0.0
    ).astype(BF16)
    weighted = (hot * tile.astype(F32)).astype(BF16)
    ids = lax.dot_general(weighted, rank_hot, NT, preferred_element_type=F32)
    ids_s[:, 0, :] = (ids + 0.5).astype(jnp.int32)
    slot_of = owner * slots + rank

    dest_blk = max(1, 128 // slots)
    while h % dest_blk:
        dest_blk //= 2
    rows = dest_blk * slots
    planes = h // dest_blk
    my_plane = mine // dest_blk
    my_place = lax.rem(mine, dest_blk)

    def plane_of(g):
        if planes & (planes - 1):
            return lax.rem(my_plane + g, planes)
        total = jnp.int32(0)
        bit = 1
        while bit < planes:
            total = total + lax.rem(my_plane // bit + g // bit, 2) * bit
            bit *= 2
        return total

    def dest_of(g, j):
        return plane_of(g) * dest_blk + lax.rem(my_place + j, dest_blk)


    pl.semaphore_wait(barrier, h)

    def wr_copy(k):
        other = lax.rem(my_brick + k, bricks)
        return pltpu.make_async_remote_copy(
            src_ref=wr_s,
            dst_ref=wrecv_s.at[my_brick],
            send_sem=wr_send_sem.at[k],
            recv_sem=wr_recv_sem.at[k],
            device_id=(my_body, other),
            device_id_type=MESH,
        )

    def start(phase, k, carry):
        d = dest_of(k // dest_blk, lax.rem(k, dest_blk))
        where = device(my_half, d)
        slot = phase * h + k
        pltpu.make_async_remote_copy(
            src_ref=send_s.at[slot],
            dst_ref=recv_s.at[slot],
            send_sem=send_sem.at[phase],
            recv_sem=recv_sem.at[slot],
            device_id=where,
            device_id_type=MESH,
        ).start()
        pltpu.make_async_remote_copy(
            src_ref=ids_s.at[phase * h + d],
            dst_ref=ids_recv_s.at[slot],
            send_sem=ids_send_sem.at[phase],
            recv_sem=ids_recv_sem.at[slot],
            device_id=where,
            device_id_type=MESH,
        ).start()
        return carry

    def pack(i, carry):
        phase = i // planes
        g = lax.rem(i + 1, planes)
        place = lax.broadcasted_iota(jnp.int32, (rows, blocks), 0) + my_place * slots
        place = jnp.where(place >= rows, place - rows, place)
        target = phase * (h * slots) + plane_of(g) * rows + place
        pick = jnp.where(target == slot_of, 1.0, 0.0).astype(BF16)
        out = jnp.dot(pick, split_s[0], preferred_element_type=F32)
        out = out + jnp.dot(pick, split_s[1], preferred_element_type=F32)
        low = lax.broadcasted_iota(jnp.int32, (8, 128), 1) < 64
        nch = slots // 8
        for d in range(dest_blk):
            k = phase * h + g * dest_blk + d
            for m in range(nch):
                r = d * slots + m * 8
                for t in range(4):
                    send_s[k, m * 4 + t] = out[r : r + 8, t * 128 : (t + 1) * 128]
            if nch % 2 == 0:
                for m in range(0, nch, 2):
                    r = d * slots + m * 8
                    send_s[k, 4 * nch + m // 2] = jnp.where(
                        low, out[r : r + 8, 512:640], out[r + 8 : r + 16, 512:640]
                    )
            else:
                for m in range(nch):
                    r = d * slots + m * 8
                    send_s[k, 4 * nch + m] = out[r : r + 8, 512:640]


        @pl.when(phase == 0)
        def _():
            least = jnp.where(g == 0, 1, 0)
            lax.fori_loop(
                g * dest_blk + least, (g + 1) * dest_blk, functools.partial(start, 0), 0
            )

        return carry

    def own_copies(phase):
        k = phase * h
        return (
            pltpu.make_async_copy(send_s.at[k], recv_s.at[k], recv_sem.at[k]),
            pltpu.make_async_copy(ids_s.at[k + mine], ids_recv_s.at[k], ids_recv_sem.at[k]),
        )

    lax.fori_loop(0, 2 * planes, pack, 0)
    for phase in range(2):
        for copy in own_copies(phase):
            copy.start()

    def wrench_part(j, wrench):
        base = pl.multiple_of(j * width, 128)
        seg = segment_matrix(group, width, base)
        live = live_s[:, pl.ds(base, width)]
        loaded = [force_ref[c, :, pl.ds(base, width)] * live for c in range(3)]
        offset = [offset_ref[c, :, pl.ds(base, width)] for c in range(3)]
        torque = cross(offset, loaded)
        sums = [jnp.sum(v, axis=0, keepdims=True) for v in loaded + list(torque)]
        sums = jnp.concatenate(sums + [jnp.zeros((2, width), F32)], axis=0)
        return wrench + lax.dot_general(stack3(sums), seg, NT, preferred_element_type=F32)

    wrench3 = lax.fori_loop(0, chunks, wrench_part, jnp.zeros((24, group), F32), unroll=8)
    wr_s[...] = wrench3[0:8] + wrench3[8:16] + wrench3[16:24]
    wrecv_s[my_brick] = wr_s[...]
    for k in range(1, bricks):
        wr_copy(k).start()

    def velocities():
        for k in range(1, bricks):
            wr_copy(k).wait()
        wrench = wrecv_s[0]
        for k in range(1, bricks):
            wrench = wrench + wrecv_s[k]
        velocity = [jnp.sum(mob_ref[i] * wrench[0:6], axis=0, keepdims=True) for i in range(6)]
        velocity = jnp.concatenate(velocity + [jnp.zeros((2, group), F32)], axis=0)
        vel3 = stack3(velocity)

        def spread_velocity(j, carry):
            base = pl.multiple_of(j * width, 128)
            seg = segment_matrix(group, width, base)
            v3 = jnp.dot(vel3, seg, preferred_element_type=F32)
            v = v3[0:8] + v3[8:16] + v3[16:24]
            live = live_s[:, pl.ds(base, width)]
            offset = [offset_ref[c, :, pl.ds(base, width)] for c in range(3)]
            spin = cross([v[3:4], v[4:5], v[5:6]], offset)
            for c in range(3):
                vel_ref[c, :, pl.ds(base, width)] = (v[c : c + 1] + spin[c]) * live
            return carry

        lax.fori_loop(0, chunks, spread_velocity, 0, unroll=8)

    nch = slots // 8
    edge = TILE_EDGE
    rows_ci = 3 * edge
    batch = dest_blk
    lanes8 = lax.broadcasted_iota(jnp.int32, (8, 128), 1)
    centre = lax.broadcasted_iota(jnp.int32, (edge, 128), 0).astype(F32) + (0.5 - edge / 2)
    pairs = slots // 2
    low_share = lax.broadcasted_iota(jnp.int32, (rows_ci, 128), 1) < edge * edge
    low = lax.broadcasted_iota(jnp.int32, (TILES_DEV, 128), 1) < edge * edge

    def unpacked(k, m):
        parts = [recv_s[k, 4 * m + t] for t in range(4)]
        if nch % 2 == 0:
            tail = recv_s[k, 4 * nch + m // 2]
            if m % 2:
                tail = pltpu.roll(tail, 64, 1)
        else:
            tail = recv_s[k, 4 * nch + m]
        parts.append(tail)
        values = []
        for c in range(6):
            first, off = divmod(c * PSLOT, 128)
            value = parts[first]
            if off:
                value = pltpu.roll(value, 128 - off, 1)
                if off + PSLOT > 128:
                    other = pltpu.roll(parts[first + 1], 128 - off, 1)
                    value = jnp.where(lanes8 < 128 - off, value, other)
            values.append(value)
        return values

    def features_of(y, z):
        level = -2.0 * LOG_ROOT - HALF_LOG * (y * y + z * z)
        features = []
        for value in (level, (2.0 * HALF_LOG) * y, (2.0 * HALF_LOG) * z):
            top = value.astype(BF16).astype(F32)
            rest = value - top
            middle = rest.astype(BF16).astype(F32)
            features += [top, middle, rest - middle]
        features.append(jnp.ones((8, 128), F32))
        features = jnp.concatenate(features, axis=0).astype(BF16)
        return jnp.swapaxes(features, 0, 1)[0:PSLOT]

    def left_of(m, r):
        row = [comp_s[m, c, r : r + 1, :] for c in range(4)]
        gap = row[3] - centre
        wx = jnp.exp2(-LOG_ROOT - HALF_LOG * (gap * gap))
        return [row[c] * wx for c in range(3)]

    def nth(i):
        other = jnp.where(i > h - dest_blk, i - (h - dest_blk), i - 1 + dest_blk)
        return jnp.where(i == 0, 0, other)

    def arrived(phase, i):
        k = phase * h + nth(i)
        pltpu.make_async_copy(recv_s.at[k], recv_s.at[k], recv_sem.at[k]).wait()
        pltpu.make_async_copy(ids_recv_s.at[k], ids_recv_s.at[k], ids_recv_sem.at[k]).wait()

    def take(phase, i):
        k = phase * h + nth(i)
        for m in range(nch):
            values = unpacked(k, m)
            for c in range(4):
                comp_s[m, c] = values[c]
            feature_s[m * PSLOT : (m + 1) * PSLOT, :] = features_of(values[4], values[5])

    def weigh():
        exponent = jnp.dot(feature_s[...], basis_ref[...], preferred_element_type=F32)
        for m in range(nch):
            for half in range(2):
                lanes = slice(half * 256, (half + 1) * 256)
                right = jnp.exp2(exponent[m * PSLOT : (m + 1) * PSLOT, lanes])
                right_hi = right.astype(BF16)
                right_s[2 * m + half, 0:PSLOT, :] = right_hi
                right_s[2 * m + half, PSLOT : 2 * PSLOT, :] = (
                    right - right_hi.astype(F32)
                ).astype(BF16)
                left = []
                for r in range(4 * half, 4 * half + 4):
                    left += left_of(m, r)
                left = jnp.concatenate(left, axis=0)
                left_hi = left.astype(BF16)
                left_lo = (left - left_hi.astype(F32)).astype(BF16)[:, 0:PSLOT]
                left_hi = left_hi[:, 0:PSLOT]
                left_s[2 * m + half, 0 : 4 * rows_ci, :] = jnp.concatenate(
                    [left_hi, left_hi], axis=1
                )
                left_s[2 * m + half, 4 * rows_ci : 8 * rows_ci, :] = jnp.concatenate(
                    [left_lo, jnp.zeros_like(left_lo)], axis=1
                )

    def spread(i):
        b = lax.rem(i, batch)
        for u in range(2 * nch):
            left = left_s[u]
            both = jnp.dot(left, right_s[u], preferred_element_type=F32)
            for t in range(2):
                lanes = slice(t * 128, (t + 1) * 128)
                at = 2 * t * rows_ci
                even = both[at : at + rows_ci, lanes]
                even = even + both[at + 4 * rows_ci : at + 5 * rows_ci, lanes]
                odd = both[at + rows_ci : at + 2 * rows_ci, lanes]
                odd = odd + both[at + 5 * rows_ci : at + 6 * rows_ci, lanes]
                to = pl.multiple_of((b * pairs + 2 * u + t) * rows_ci, 8)
                share_s[pl.ds(to, rows_ci), :] = jnp.where(low_share, even, odd)

    def gather_tiles(phase, i, finish=None):
        count = batch * pairs
        names = jnp.zeros((1, 128), jnp.int32)
        for b in range(batch):
            k = phase * h + nth(i - (batch - 1) + b)
            row = ids_recv_s[k]
            names = names + (pltpu.roll(row, b * pairs, 1) if b else row)
        tile_of = lax.broadcasted_iota(jnp.int32, (TILES_DEV, 128), 0)
        hot_tile = jnp.concatenate(
            [
                jnp.where(tile_of == names, 1.0, 0.0)[:, 0:count],
                jnp.where(tile_of == pltpu.roll(names, 64, 1), 1.0, 0.0)[:, 0:count],
            ],
            axis=0,
        ).astype(BF16)
        for r in range(rows_ci):
            share = share_s[pl.ds(r, count, stride=rows_ci), :]
            share_hi = share.astype(BF16)
            share_lo = (share - share_hi.astype(F32)).astype(BF16)
            gained = jnp.dot(hot_tile, share_hi, preferred_element_type=F32)
            gained = gained + jnp.dot(hot_tile, share_lo, preferred_element_type=F32)
            total_s[r] = total_s[r] + jnp.where(low, gained[0:TILES_DEV], gained[TILES_DEV:])
            if finish is not None and r % edge == edge - 1:
                finish(r // edge)

    def receive(phase, finish):
        total_s[...] = jnp.zeros_like(total_s)
        arrived(phase, 0)
        take(phase, 0)
        arrived(phase, 1)
        weigh()
        take(phase, 1)

        def step(i, carry):
            arrived(phase, i)
            spread(i - 2)
            weigh()
            take(phase, i)

            @pl.when(lax.rem(i - 2, batch) == batch - 1)
            def _():
                gather_tiles(phase, i - 2)

            return carry

        lax.fori_loop(2, h, step, 0)
        spread(h - 2)
        weigh()
        spread(h - 1)
        gather_tiles(phase, h - 1, finish)

    def folded(c, i):
        even = total_s[c * edge + i]
        odd = total_s[c * edge + i + 1]
        even = even + pltpu.roll(even, 64, 1)
        odd = odd + pltpu.roll(odd, 64, 1)
        return jnp.where(low, even, odd)

    def far_copy(c):
        return pltpu.make_async_remote_copy(
            src_ref=far_s.at[c],
            dst_ref=far_recv_s.at[c],
            send_sem=far_send_sem.at[c],
            recv_sem=far_recv_sem.at[c],
            device_id=mirror,
            device_id_type=MESH,
        )

    def send_far(c):
        for i in range(0, edge, 2):
            far_s[c, :, i * 64 : i * 64 + 128] = folded(c, i)
        far_copy(c).start()

    def write_grid(c):
        for i in range(0, edge, 2):
            grid_ref[c, :, i * 64 : i * 64 + 128] = folded(c, i)

    velocities()
    lax.fori_loop(dest_blk, h, functools.partial(start, 1), 0)
    lax.fori_loop(1, dest_blk, functools.partial(start, 1), 0)
    receive(0, send_far)
    receive(1, write_grid)
    for c in range(3):
        far_copy(c).wait()
        grid_ref[c] = grid_ref[c] + far_recv_s[c]

    for phase in range(2):
        rest = send_s.at[pl.ds(phase * h + 1, h - 1)]
        pltpu.make_async_copy(rest, rest, send_sem.at[phase]).wait()
        rest_ids = ids_s.at[pl.ds(phase * h + 1, h - 1)]
        pltpu.make_async_copy(rest_ids, rest_ids, ids_send_sem.at[phase]).wait()


def body(
    blob_force, blob_offset, patch_anchor, patch_count, block_owner, block_tile, body_mobility
):
    edge = TILE_EDGE
    lp = blob_force.shape[1]
    group = body_mobility.shape[2]
    length = group * PSLOT
    bodies = lax.axis_size("body")
    bricks = lax.axis_size("brick")
    n = bodies * bricks
    capacity = max(2, 2 * group // n)
    slots = -(-lp * capacity // 8) * 8
    nch = slots // 8
    tiles = 4 * nch + (nch // 2 if nch % 2 == 0 else nch)
    blocks = lp * group
    width = 768
    rpad = -(-4 * lp // 8) * 8
    batch = max(1, 128 // slots)
    while (n // 2) % batch:
        batch //= 2
    dims = (bodies, bricks, lp, group, width, slots, tiles)
    limit = (16 << 20) + 2 * n * (tiles + 1) * 4096
    vmem = pl.BlockSpec(memory_space=pltpu.VMEM)
    velocity, grid = pl.pallas_call(
        functools.partial(step_kernel, dims),
        name="step",
        out_shape=(
            jax.ShapeDtypeStruct((3, lp, length), F32),
            jax.ShapeDtypeStruct((3, TILES_DEV, edge**3), F32),
        ),
        in_specs=[pl.BlockSpec(memory_space=pltpu.HBM)] * 8,
        out_specs=(vmem, vmem),
        scratch_shapes=[
            pltpu.VMEM((rpad, group), F32),
            pltpu.VMEM((2, blocks), jnp.int32),
            pltpu.VMEM((lp, length), F32),
            pltpu.VMEM((6, lp, width), F32),
            pltpu.VMEM((lp, 8, 640), F32),
            pltpu.VMEM((lp, group, 640), F32),
            pltpu.VMEM((2, blocks, 640), BF16),
            pltpu.VMEM((n, tiles, 8, 128), F32),
            pltpu.VMEM((n, 1, 128), jnp.int32),
            pltpu.VMEM((n, tiles, 8, 128), F32),
            pltpu.VMEM((n, 1, 128), jnp.int32),
            pltpu.VMEM((nch, 4, 8, 128), F32),
            pltpu.VMEM((nch * PSLOT, 80), BF16),
            pltpu.VMEM((2 * nch, 2 * PSLOT, 4 * edge * edge), BF16),
            pltpu.VMEM((2 * nch, 24 * edge, 2 * PSLOT), BF16),
            pltpu.VMEM((batch * slots // 2 * 3 * edge, 128), F32),
            pltpu.VMEM((3 * edge, TILES_DEV, 128), F32),
            pltpu.VMEM((8, group), F32),
            pltpu.VMEM((bricks, 8, group), F32),
            pltpu.VMEM((3, TILES_DEV, edge**3), F32),
            pltpu.VMEM((3, TILES_DEV, edge**3), F32),
            pltpu.SemaphoreType.DMA((2,)),
            pltpu.SemaphoreType.DMA((n,)),
            pltpu.SemaphoreType.DMA((2,)),
            pltpu.SemaphoreType.DMA((n,)),
            pltpu.SemaphoreType.DMA((bricks,)),
            pltpu.SemaphoreType.DMA((bricks,)),
            pltpu.SemaphoreType.DMA((3,)),
            pltpu.SemaphoreType.DMA((3,)),
            pltpu.VMEM((3, lp, length), F32),
            pltpu.VMEM((3, lp, length), F32),
            pltpu.VMEM((3, lp, group), F32),
            pltpu.VMEM((lp, group), jnp.int32),
            pltpu.VMEM((lp, 1, group), jnp.int32),
            pltpu.VMEM((lp, group), jnp.int32),
            pltpu.VMEM((6, 6, group), F32),
            pltpu.VMEM((80, 8 * edge * edge), BF16),
            pltpu.SemaphoreType.DMA((8,)),
        ],
        compiler_params=pltpu.CompilerParams(
            collective_id=0, has_side_effects=True, vmem_limit_bytes=limit
        ),
    )(*[
        pltpu.with_memory_space_constraint(x, pltpu.HBM)
        for x in (
            blob_force,
            blob_offset,
            patch_anchor,
            jnp.transpose(patch_count),
            jnp.transpose(block_owner, (0, 2, 1)),
            block_tile,
            body_mobility,
            jnp.asarray(exponent_basis(edge)),
        )
    ])
    return velocity, jnp.transpose(grid, (1, 0, 2))


def solution(mesh):
    in_specs = (
        P(None, "brick", "body"),
        P(None, "brick", "body"),
        P(None, "brick", "body"),
        P("body", "brick"),
        P("brick", "body", None),
        P("brick", "body"),
        P(None, None, "body"),
    )
    out_specs = (P(None, "brick", "body"), P(("body", "brick"), None, None))
    return jax.shard_map(body, mesh=mesh, in_specs=in_specs, out_specs=out_specs, check_vma=False)
```

```python
import functools
import math

import jax
import jax.numpy as jnp
import ml_dtypes
import numpy as np
from jax import lax
from jax.experimental import pallas as pl
from jax.experimental.pallas import tpu as pltpu
from jax.sharding import PartitionSpec as P

PSLOT = 96
TILE_EDGE = 8
TILES_DEV = 32
LOG_ROOT = 0.5 * math.log2(2.0 * math.pi)
HALF_LOG = 0.5 / math.log(2.0)
MESH = pl.DeviceIdType.MESH
NT = (((1,), (1,)), ((), ()))
F32 = jnp.float32
BF16 = jnp.bfloat16


def stack3(x):
    hi = x.astype(BF16).astype(F32)
    rest = x - hi
    mid = rest.astype(BF16).astype(F32)
    lo = rest - mid
    return jnp.concatenate([hi, mid, lo], axis=0).astype(BF16)


def cross(left, right):
    return (
        left[1] * right[2] - left[2] * right[1],
        left[2] * right[0] - left[0] * right[2],
        left[0] * right[1] - left[1] * right[0],
    )


def segment_matrix(group, width, base):
    lane = lax.broadcasted_iota(jnp.int32, (group, width), 1) + base
    start = lax.broadcasted_iota(jnp.int32, (group, width), 0) * PSLOT
    gap = lane - start
    return jnp.where((gap >= 0) & (gap < PSLOT), 1.0, 0.0).astype(BF16)


def exponent_basis(edge):
    cells = edge * edge
    centre = np.arange(edge, dtype=np.float32) + 0.5 - edge / 2
    first = np.repeat(centre, edge)
    second = np.tile(centre, edge)
    basis = np.zeros((80, 8, cells), np.float32)
    for slot in range(8):
        for part in range(3):
            basis[8 * part + slot, slot] = 1.0
            basis[24 + 8 * part + slot, slot] = first
            basis[48 + 8 * part + slot, slot] = second
    rest = (-HALF_LOG * (first**2 + second**2)).astype(np.float32)
    for part in range(3):
        top = rest.astype(ml_dtypes.bfloat16).astype(np.float32)
        basis[72 + part, :] = top
        rest = rest - top
    return basis.reshape(80, 8 * cells).astype(ml_dtypes.bfloat16)


def step_kernel(
    dims,
    force_hbm,
    offset_hbm,
    anchor_hbm,
    count_hbm,
    owner_hbm,
    tile_hbm,
    mob_hbm,
    basis_hbm,
    vel_ref,
    grid_ref,
    rows_s,
    meta_s,
    live_s,
    flat_s,
    turn_s,
    data_s,
    split_s,
    send_s,
    ids_s,
    recv_s,
    ids_recv_s,
    comp_s,
    feature_s,
    right_s,
    left_s,
    share_s,
    total_s,
    wr_s,
    wrecv_s,
    far_s,
    far_recv_s,
    send_sem,
    recv_sem,
    ids_send_sem,
    ids_recv_sem,
    wr_send_sem,
    wr_recv_sem,
    far_send_sem,
    far_recv_sem,
    force_ref,
    offset_ref,
    anchor_ref,
    count_ref,
    owner_ref,
    tile_ref,
    mob_ref,
    basis_ref,
    in_sem,
):
    bodies, bricks, lp, group, width, slots, tiles = dims
    n = bodies * bricks
    h = n // 2
    turn = h // 2 if h % 2 == 0 else 0
    length = group * PSLOT
    chunks = length // width
    per = width // PSLOT
    rpad = rows_s.shape[0]
    blocks = lp * group
    my_body = lax.axis_index("body")
    my_brick = lax.axis_index("brick")
    me = my_body * bricks + my_brick
    my_half = me // h
    mine = lax.rem(me, h)

    def device(half, place):
        d = half * h + place
        return (d // bricks, lax.rem(d, bricks))

    mirror = device(1 - my_half, lax.rem(mine + turn, h))

    loads = [
        pltpu.make_async_copy(source, target, in_sem.at[i])
        for i, (source, target) in enumerate(
            (
                (force_hbm, force_ref),
                (offset_hbm, offset_ref),
                (anchor_hbm, anchor_ref),
                (count_hbm, count_ref),
                (owner_hbm, owner_ref),
                (tile_hbm, tile_ref),
                (mob_hbm, mob_ref),
                (basis_hbm, basis_ref),
            )
        )
    ]
    for load in loads:
        load.start()

    barrier = pltpu.get_barrier_semaphore()

    def greet(k, carry):
        pl.semaphore_signal(
            barrier,
            inc=1,
            device_id=device(my_half, lax.rem(mine + k, h)),
            device_id_type=MESH,
        )
        return carry

    pl.semaphore_signal(barrier, inc=1, device_id=mirror, device_id_type=MESH)
    lax.fori_loop(1, h, greet, 0)

    for load in loads[:6]:
        load.wait()
    rows_s[...] = jnp.zeros_like(rows_s)
    for c in range(3):
        rows_s[c * lp : (c + 1) * lp, :] = anchor_ref[c] - TILE_EDGE / 2
    starts = PSLOT * lax.broadcasted_iota(jnp.int32, (lp, group), 1)
    rows_s[3 * lp : 4 * lp, :] = (count_ref[...] + starts).astype(F32)
    for q in range(lp):
        meta_s[0:1, q * group : (q + 1) * group] = owner_ref[q]
        meta_s[1:2, q * group : (q + 1) * group] = tile_ref[q : q + 1, :]
    rows3 = stack3(rows_s[...])

    def chunk(j, carry):
        base = pl.multiple_of(j * width, 128)
        seg = segment_matrix(group, width, base)
        flat3 = jnp.dot(rows3, seg, preferred_element_type=F32)
        flat = flat3[0:rpad] + flat3[rpad : 2 * rpad] + flat3[2 * rpad : 3 * rpad]
        lane = (lax.broadcasted_iota(jnp.int32, (lp, width), 1) + base).astype(F32)
        live = jnp.where(lane < flat[3 * lp : 4 * lp], 1.0, 0.0)
        live_s[:, pl.ds(base, width)] = live
        loaded = [force_ref[c, :, pl.ds(base, width)] * live for c in range(3)]
        offset = [offset_ref[c, :, pl.ds(base, width)] for c in range(3)]
        for c in range(3):
            flat_s[c] = loaded[c]
            flat_s[3 + c] = offset[c] + flat[c * lp : (c + 1) * lp]
        for m in range(per):
            for c in range(6):
                piece = flat_s[c, :, m * PSLOT : (m + 1) * PSLOT]
                for q in range(lp):
                    turn_s[q, m : m + 1, c * PSLOT : (c + 1) * PSLOT] = piece[q : q + 1]
        data_s[:, pl.ds(pl.multiple_of(j * per, per), per), :] = turn_s[...]
        return carry

    lax.fori_loop(0, chunks, chunk, 0, unroll=8)

    data = data_s[...].reshape(blocks, 640)
    tail = data[:, 512:576]
    data = jnp.concatenate([data[:, 0:512], tail, tail], axis=1)
    data_hi = data.astype(BF16)
    split_s[0] = data_hi
    split_s[1] = (data - data_hi.astype(F32)).astype(BF16)

    owner = meta_s[0:1, :]
    tile = meta_s[1:2, :]
    place = lax.rem(owner, h)
    proxy = place + turn
    proxy = jnp.where(proxy >= h, proxy - h, proxy)
    owner = jnp.where(owner // h == my_half, place + h, proxy)
    is_owner = lax.broadcasted_iota(jnp.int32, (n, blocks), 0) == owner
    hot = jnp.where(is_owner, 1.0, 0.0)
    before = jnp.where(
        lax.broadcasted_iota(jnp.int32, (blocks, blocks), 0)
        < lax.broadcasted_iota(jnp.int32, (blocks, blocks), 1),
        1.0,
        0.0,
    ).astype(BF16)
    seen = jnp.dot(hot.astype(BF16), before, preferred_element_type=F32)
    rank = jnp.sum(hot * seen, axis=0, keepdims=True)
    rank = (rank + 0.5).astype(jnp.int32)
    lane_of = rank // 2 + 64 * lax.rem(rank, 2)
    rank_hot = jnp.where(
        lax.broadcasted_iota(jnp.int32, (128, blocks), 0) == lane_of, 1.0, 0.0
    ).astype(BF16)
    weighted = (hot * tile.astype(F32)).astype(BF16)
    ids = lax.dot_general(weighted, rank_hot, NT, preferred_element_type=F32)
    ids_s[:, 0, :] = (ids + 0.5).astype(jnp.int32)
    slot_of = owner * slots + rank

    dest_blk = max(1, 128 // slots)
    while h % dest_blk:
        dest_blk //= 2
    rows = dest_blk * slots
    planes = h // dest_blk
    my_plane = mine // dest_blk
    my_place = lax.rem(mine, dest_blk)

    def plane_of(g):
        if planes & (planes - 1):
            return lax.rem(my_plane + g, planes)
        total = jnp.int32(0)
        bit = 1
        while bit < planes:
            total = total + lax.rem(my_plane // bit + g // bit, 2) * bit
            bit *= 2
        return total

    def dest_of(g, j):
        return plane_of(g) * dest_blk + lax.rem(my_place + j, dest_blk)


    pl.semaphore_wait(barrier, h)

    def wr_copy(k):
        other = lax.rem(my_brick + k, bricks)
        return pltpu.make_async_remote_copy(
            src_ref=wr_s,
            dst_ref=wrecv_s.at[my_brick],
            send_sem=wr_send_sem.at[k],
            recv_sem=wr_recv_sem.at[k],
            device_id=(my_body, other),
            device_id_type=MESH,
        )

    def start(phase, k, carry):
        d = dest_of(k // dest_blk, lax.rem(k, dest_blk))
        where = device(my_half, d)
        slot = phase * h + k
        pltpu.make_async_remote_copy(
            src_ref=send_s.at[slot],
            dst_ref=recv_s.at[slot],
            send_sem=send_sem.at[phase],
            recv_sem=recv_sem.at[slot],
            device_id=where,
            device_id_type=MESH,
        ).start()
        pltpu.make_async_remote_copy(
            src_ref=ids_s.at[phase * h + d],
            dst_ref=ids_recv_s.at[slot],
            send_sem=ids_send_sem.at[phase],
            recv_sem=ids_recv_sem.at[slot],
            device_id=where,
            device_id_type=MESH,
        ).start()
        return carry

    def pack(i, carry):
        phase = i // planes
        g = lax.rem(i + 1, planes)
        place = lax.broadcasted_iota(jnp.int32, (rows, blocks), 0) + my_place * slots
        place = jnp.where(place >= rows, place - rows, place)
        target = phase * (h * slots) + plane_of(g) * rows + place
        pick = jnp.where(target == slot_of, 1.0, 0.0).astype(BF16)
        out = jnp.dot(pick, split_s[0], preferred_element_type=F32)
        out = out + jnp.dot(pick, split_s[1], preferred_element_type=F32)
        low = lax.broadcasted_iota(jnp.int32, (8, 128), 1) < 64
        nch = slots // 8
        for d in range(dest_blk):
            k = phase * h + g * dest_blk + d
            for m in range(nch):
                r = d * slots + m * 8
                for t in range(4):
                    send_s[k, m * 4 + t] = out[r : r + 8, t * 128 : (t + 1) * 128]
            if nch % 2 == 0:
                for m in range(0, nch, 2):
                    r = d * slots + m * 8
                    send_s[k, 4 * nch + m // 2] = jnp.where(
                        low, out[r : r + 8, 512:640], out[r + 8 : r + 16, 512:640]
                    )
            else:
                for m in range(nch):
                    r = d * slots + m * 8
                    send_s[k, 4 * nch + m] = out[r : r + 8, 512:640]


        @pl.when(phase == 0)
        def _():
            least = jnp.where(g == 0, 1, 0)
            lax.fori_loop(
                g * dest_blk + least, (g + 1) * dest_blk, functools.partial(start, 0), 0
            )

        return carry

    def own_copies(phase):
        k = phase * h
        return (
            pltpu.make_async_copy(send_s.at[k], recv_s.at[k], recv_sem.at[k]),
            pltpu.make_async_copy(ids_s.at[k + mine], ids_recv_s.at[k], ids_recv_sem.at[k]),
        )

    lax.fori_loop(0, 2 * planes, pack, 0)
    for phase in range(2):
        for copy in own_copies(phase):
            copy.start()

    def wrench_part(j, wrench):
        base = pl.multiple_of(j * width, 128)
        seg = segment_matrix(group, width, base)
        live = live_s[:, pl.ds(base, width)]
        loaded = [force_ref[c, :, pl.ds(base, width)] * live for c in range(3)]
        offset = [offset_ref[c, :, pl.ds(base, width)] for c in range(3)]
        torque = cross(offset, loaded)
        sums = [jnp.sum(v, axis=0, keepdims=True) for v in loaded + list(torque)]
        sums = jnp.concatenate(sums + [jnp.zeros((2, width), F32)], axis=0)
        return wrench + lax.dot_general(stack3(sums), seg, NT, preferred_element_type=F32)

    wrench3 = lax.fori_loop(0, chunks, wrench_part, jnp.zeros((24, group), F32), unroll=8)
    wr_s[...] = wrench3[0:8] + wrench3[8:16] + wrench3[16:24]
    wrecv_s[my_brick] = wr_s[...]
    for k in range(1, bricks):
        wr_copy(k).start()

    def velocities():
        for k in range(1, bricks):
            wr_copy(k).wait()
        wrench = wrecv_s[0]
        for k in range(1, bricks):
            wrench = wrench + wrecv_s[k]
        velocity = [jnp.sum(mob_ref[i] * wrench[0:6], axis=0, keepdims=True) for i in range(6)]
        velocity = jnp.concatenate(velocity + [jnp.zeros((2, group), F32)], axis=0)
        vel3 = stack3(velocity)

        def spread_velocity(j, carry):
            base = pl.multiple_of(j * width, 128)
            seg = segment_matrix(group, width, base)
            v3 = jnp.dot(vel3, seg, preferred_element_type=F32)
            v = v3[0:8] + v3[8:16] + v3[16:24]
            live = live_s[:, pl.ds(base, width)]
            offset = [offset_ref[c, :, pl.ds(base, width)] for c in range(3)]
            spin = cross([v[3:4], v[4:5], v[5:6]], offset)
            for c in range(3):
                vel_ref[c, :, pl.ds(base, width)] = (v[c : c + 1] + spin[c]) * live
            return carry

        lax.fori_loop(0, chunks, spread_velocity, 0, unroll=8)

    nch = slots // 8
    edge = TILE_EDGE
    rows_ci = 3 * edge
    batch = dest_blk
    lanes8 = lax.broadcasted_iota(jnp.int32, (8, 128), 1)
    centre = lax.broadcasted_iota(jnp.int32, (edge, 128), 0).astype(F32) + (0.5 - edge / 2)
    pairs = slots // 2
    low_share = lax.broadcasted_iota(jnp.int32, (rows_ci, 128), 1) < edge * edge
    low = lax.broadcasted_iota(jnp.int32, (TILES_DEV, 128), 1) < edge * edge

    def unpacked(k, m):
        parts = [recv_s[k, 4 * m + t] for t in range(4)]
        if nch % 2 == 0:
            tail = recv_s[k, 4 * nch + m // 2]
            if m % 2:
                tail = pltpu.roll(tail, 64, 1)
        else:
            tail = recv_s[k, 4 * nch + m]
        parts.append(tail)
        values = []
        for c in range(6):
            first, off = divmod(c * PSLOT, 128)
            value = parts[first]
            if off:
                value = pltpu.roll(value, 128 - off, 1)
                if off + PSLOT > 128:
                    other = pltpu.roll(parts[first + 1], 128 - off, 1)
                    value = jnp.where(lanes8 < 128 - off, value, other)
            values.append(value)
        return values

    def features_of(y, z):
        level = -2.0 * LOG_ROOT - HALF_LOG * (y * y + z * z)
        features = []
        for value in (level, (2.0 * HALF_LOG) * y, (2.0 * HALF_LOG) * z):
            top = value.astype(BF16).astype(F32)
            rest = value - top
            middle = rest.astype(BF16).astype(F32)
            features += [top, middle, rest - middle]
        features.append(jnp.ones((8, 128), F32))
        features = jnp.concatenate(features, axis=0).astype(BF16)
        return jnp.swapaxes(features, 0, 1)[0:PSLOT]

    def left_of(m, r):
        row = [comp_s[m, c, r : r + 1, :] for c in range(4)]
        gap = row[3] - centre
        wx = jnp.exp2(-LOG_ROOT - HALF_LOG * (gap * gap))
        return [row[c] * wx for c in range(3)]

    def nth(i):
        other = jnp.where(i > h - dest_blk, i - (h - dest_blk), i - 1 + dest_blk)
        return jnp.where(i == 0, 0, other)

    def arrived(phase, i):
        k = phase * h + nth(i)
        pltpu.make_async_copy(recv_s.at[k], recv_s.at[k], recv_sem.at[k]).wait()
        pltpu.make_async_copy(ids_recv_s.at[k], ids_recv_s.at[k], ids_recv_sem.at[k]).wait()

    def take(phase, i):
        k = phase * h + nth(i)
        for m in range(nch):
            values = unpacked(k, m)
            for c in range(4):
                comp_s[m, c] = values[c]
            feature_s[m * PSLOT : (m + 1) * PSLOT, :] = features_of(values[4], values[5])

    def weigh():
        exponent = jnp.dot(feature_s[...], basis_ref[...], preferred_element_type=F32)
        for m in range(nch):
            for half in range(2):
                lanes = slice(half * 256, (half + 1) * 256)
                right = jnp.exp2(exponent[m * PSLOT : (m + 1) * PSLOT, lanes])
                right_hi = right.astype(BF16)
                right_s[2 * m + half, 0:PSLOT, :] = right_hi
                right_s[2 * m + half, PSLOT : 2 * PSLOT, :] = (
                    right - right_hi.astype(F32)
                ).astype(BF16)
                left = []
                for r in range(4 * half, 4 * half + 4):
                    left += left_of(m, r)
                left = jnp.concatenate(left, axis=0)
                left_hi = left.astype(BF16)
                left_lo = (left - left_hi.astype(F32)).astype(BF16)[:, 0:PSLOT]
                left_hi = left_hi[:, 0:PSLOT]
                left_s[2 * m + half, 0 : 4 * rows_ci, :] = jnp.concatenate(
                    [left_hi, left_hi], axis=1
                )
                left_s[2 * m + half, 4 * rows_ci : 8 * rows_ci, :] = jnp.concatenate(
                    [left_lo, jnp.zeros_like(left_lo)], axis=1
                )

    def spread(i):
        b = lax.rem(i, batch)
        for u in range(2 * nch):
            left = left_s[u]
            both = jnp.dot(left, right_s[u], preferred_element_type=F32)
            for t in range(2):
                lanes = slice(t * 128, (t + 1) * 128)
                at = 2 * t * rows_ci
                even = both[at : at + rows_ci, lanes]
                even = even + both[at + 4 * rows_ci : at + 5 * rows_ci, lanes]
                odd = both[at + rows_ci : at + 2 * rows_ci, lanes]
                odd = odd + both[at + 5 * rows_ci : at + 6 * rows_ci, lanes]
                to = pl.multiple_of((b * pairs + 2 * u + t) * rows_ci, 8)
                share_s[pl.ds(to, rows_ci), :] = jnp.where(low_share, even, odd)

    def gather_tiles(phase, i, finish=None):
        count = batch * pairs
        names = jnp.zeros((1, 128), jnp.int32)
        for b in range(batch):
            k = phase * h + nth(i - (batch - 1) + b)
            row = ids_recv_s[k]
            names = names + (pltpu.roll(row, b * pairs, 1) if b else row)
        tile_of = lax.broadcasted_iota(jnp.int32, (TILES_DEV, 128), 0)
        hot_tile = jnp.concatenate(
            [
                jnp.where(tile_of == names, 1.0, 0.0)[:, 0:count],
                jnp.where(tile_of == pltpu.roll(names, 64, 1), 1.0, 0.0)[:, 0:count],
            ],
            axis=0,
        ).astype(BF16)
        for r in range(rows_ci):
            share = share_s[pl.ds(r, count, stride=rows_ci), :]
            share_hi = share.astype(BF16)
            share_lo = (share - share_hi.astype(F32)).astype(BF16)
            gained = jnp.dot(hot_tile, share_hi, preferred_element_type=F32)
            gained = gained + jnp.dot(hot_tile, share_lo, preferred_element_type=F32)
            total_s[r] = total_s[r] + jnp.where(low, gained[0:TILES_DEV], gained[TILES_DEV:])
            if finish is not None and r % edge == edge - 1:
                finish(r // edge)

    def receive(phase, finish):
        total_s[...] = jnp.zeros_like(total_s)
        arrived(phase, 0)
        take(phase, 0)
        arrived(phase, 1)
        weigh()
        take(phase, 1)

        def step(i, carry):
            arrived(phase, i)
            spread(i - 2)
            weigh()
            take(phase, i)

            @pl.when(lax.rem(i - 2, batch) == batch - 1)
            def _():
                gather_tiles(phase, i - 2)

            return carry

        lax.fori_loop(2, h, step, 0)
        spread(h - 2)
        weigh()
        spread(h - 1)
        gather_tiles(phase, h - 1, finish)

    def folded(c, i):
        even = total_s[c * edge + i]
        odd = total_s[c * edge + i + 1]
        even = even + pltpu.roll(even, 64, 1)
        odd = odd + pltpu.roll(odd, 64, 1)
        return jnp.where(low, even, odd)

    def far_copy(c):
        return pltpu.make_async_remote_copy(
            src_ref=far_s.at[c],
            dst_ref=far_recv_s.at[c],
            send_sem=far_send_sem.at[c],
            recv_sem=far_recv_sem.at[c],
            device_id=mirror,
            device_id_type=MESH,
        )

    def send_far(c):
        for i in range(0, edge, 2):
            far_s[c, :, i * 64 : i * 64 + 128] = folded(c, i)
        far_copy(c).start()

    def write_grid(c):
        for i in range(0, edge, 2):
            grid_ref[c, :, i * 64 : i * 64 + 128] = folded(c, i)

    for load in loads[6:]:
        load.wait()
    velocities()
    lax.fori_loop(dest_blk, h, functools.partial(start, 1), 0)
    lax.fori_loop(1, dest_blk, functools.partial(start, 1), 0)
    receive(0, send_far)
    receive(1, write_grid)
    for c in range(3):
        far_copy(c).wait()
        grid_ref[c] = grid_ref[c] + far_recv_s[c]

    for phase in range(2):
        rest = send_s.at[pl.ds(phase * h + 1, h - 1)]
        pltpu.make_async_copy(rest, rest, send_sem.at[phase]).wait()
        rest_ids = ids_s.at[pl.ds(phase * h + 1, h - 1)]
        pltpu.make_async_copy(rest_ids, rest_ids, ids_send_sem.at[phase]).wait()


def body(
    blob_force, blob_offset, patch_anchor, patch_count, block_owner, block_tile, body_mobility
):
    edge = TILE_EDGE
    lp = blob_force.shape[1]
    group = body_mobility.shape[2]
    length = group * PSLOT
    bodies = lax.axis_size("body")
    bricks = lax.axis_size("brick")
    n = bodies * bricks
    capacity = max(2, 2 * group // n)
    slots = -(-lp * capacity // 8) * 8
    nch = slots // 8
    tiles = 4 * nch + (nch // 2 if nch % 2 == 0 else nch)
    blocks = lp * group
    width = 768
    rpad = -(-4 * lp // 8) * 8
    batch = max(1, 128 // slots)
    while (n // 2) % batch:
        batch //= 2
    dims = (bodies, bricks, lp, group, width, slots, tiles)
    limit = (16 << 20) + 2 * n * (tiles + 1) * 4096
    vmem = pl.BlockSpec(memory_space=pltpu.VMEM)
    velocity, grid = pl.pallas_call(
        functools.partial(step_kernel, dims),
        name="step",
        out_shape=(
            jax.ShapeDtypeStruct((3, lp, length), F32),
            jax.ShapeDtypeStruct((3, TILES_DEV, edge**3), F32),
        ),
        in_specs=[pl.BlockSpec(memory_space=pltpu.HBM)] * 8,
        out_specs=(vmem, vmem),
        scratch_shapes=[
            pltpu.VMEM((rpad, group), F32),
            pltpu.VMEM((2, blocks), jnp.int32),
            pltpu.VMEM((lp, length), F32),
            pltpu.VMEM((6, lp, width), F32),
            pltpu.VMEM((lp, 8, 640), F32),
            pltpu.VMEM((lp, group, 640), F32),
            pltpu.VMEM((2, blocks, 640), BF16),
            pltpu.VMEM((n, tiles, 8, 128), F32),
            pltpu.VMEM((n, 1, 128), jnp.int32),
            pltpu.VMEM((n, tiles, 8, 128), F32),
            pltpu.VMEM((n, 1, 128), jnp.int32),
            pltpu.VMEM((nch, 4, 8, 128), F32),
            pltpu.VMEM((nch * PSLOT, 80), BF16),
            pltpu.VMEM((2 * nch, 2 * PSLOT, 4 * edge * edge), BF16),
            pltpu.VMEM((2 * nch, 24 * edge, 2 * PSLOT), BF16),
            pltpu.VMEM((batch * slots // 2 * 3 * edge, 128), F32),
            pltpu.VMEM((3 * edge, TILES_DEV, 128), F32),
            pltpu.VMEM((8, group), F32),
            pltpu.VMEM((bricks, 8, group), F32),
            pltpu.VMEM((3, TILES_DEV, edge**3), F32),
            pltpu.VMEM((3, TILES_DEV, edge**3), F32),
            pltpu.SemaphoreType.DMA((2,)),
            pltpu.SemaphoreType.DMA((n,)),
            pltpu.SemaphoreType.DMA((2,)),
            pltpu.SemaphoreType.DMA((n,)),
            pltpu.SemaphoreType.DMA((bricks,)),
            pltpu.SemaphoreType.DMA((bricks,)),
            pltpu.SemaphoreType.DMA((3,)),
            pltpu.SemaphoreType.DMA((3,)),
            pltpu.VMEM((3, lp, length), F32),
            pltpu.VMEM((3, lp, length), F32),
            pltpu.VMEM((3, lp, group), F32),
            pltpu.VMEM((lp, group), jnp.int32),
            pltpu.VMEM((lp, 1, group), jnp.int32),
            pltpu.VMEM((lp, group), jnp.int32),
            pltpu.VMEM((6, 6, group), F32),
            pltpu.VMEM((80, 8 * edge * edge), BF16),
            pltpu.SemaphoreType.DMA((8,)),
        ],
        compiler_params=pltpu.CompilerParams(
            collective_id=0, has_side_effects=True, vmem_limit_bytes=limit
        ),
    )(*[
        pltpu.with_memory_space_constraint(x, pltpu.HBM)
        for x in (
            blob_force,
            blob_offset,
            patch_anchor,
            jnp.transpose(patch_count),
            jnp.transpose(block_owner, (0, 2, 1)),
            block_tile,
            body_mobility,
            jnp.asarray(exponent_basis(edge)),
        )
    ])
    return velocity, jnp.transpose(grid, (1, 0, 2))


def solution(mesh):
    in_specs = (
        P(None, "brick", "body"),
        P(None, "brick", "body"),
        P(None, "brick", "body"),
        P("body", "brick"),
        P("brick", "body", None),
        P("brick", "body"),
        P(None, None, "body"),
    )
    out_specs = (P(None, "brick", "body"), P(("body", "brick"), None, None))
    return jax.shard_map(body, mesh=mesh, in_specs=in_specs, out_specs=out_specs, check_vma=False)
```
